512 devices in a mesh: dp: 16 (over x_lo, y, core), seq: 32 (over z, x_hi).
Axes of the slice: x: 4 (x_hi: 2, x_lo: 2; x = x_hi * 2 + x_lo), y: 4, z: 16, core: 2. Of those that a mesh axis runs over, the one named last changes fastest.
Arguments:
- tokens: bfloat16 [8192, 6144], P('seq'), may hold values from -6 to 6
- qkv_weight: bfloat16 [6144, 3, 4096], P('seq', None, 'dp'), may hold values from -0.078125 to 0.078125
- out_weight: bfloat16 [6144, 4096], P('seq', 'dp'), may hold values from -0.1875 to 0.1875
- log_decay: float32 [32, 8192], P('dp', 'seq'), may hold values from -1.5 to 0, as said below
- norm_gain: float32 [4096], P('dp'), may hold values from 0.25 to 1.75
Outputs:
- mixed: bfloat16 [8192, 6144], P('seq', 'dp')
The draws below stay inside these ranges and needn't reach their ends.
Inputs may be any that keep to these rules, and one draw needn't show every extreme that they name: `log_decay`: each entry is the logarithm of one head's decay factor at one position.
All inputs are finite; a program needn't handle non-finite values.
Results may differ from the reference program's by a relative error of at most 0.023.
Values may be sent and summed in bfloat16 or wider, within the bound.
No kernel may reach another device: no remote copies, remote signals or barrier semaphores. Data moves between devices by JAX's collectives and lax.ppermute only.
A program may use at most 64 MiB of HBM per device.

```python
import math
import jax
import jax.numpy as jnp
from jax import lax

D = 6144
HD = 128
HEADS = 32
TOKENS_PER_SHARD = 256
TOKENS = 8192
N_DP = 16


def draw_log_decay(key, part):
    keys = jax.random.split(jax.random.fold_in(key, 71), 6)
    share_fast = 0.5
    fast = jax.random.uniform(keys[0], (HEADS,), jnp.float32) < share_fast
    fast_rate = jnp.exp(jax.random.uniform(keys[1], (HEADS,), jnp.float32, math.log(1.0 / 50.0), math.log(1.0 / 30.0)))
    slow_decay_rate = jnp.exp(jax.random.uniform(keys[2], (HEADS,), jnp.float32, math.log(0.1), math.log(0.6))) / TOKENS
    rate = jnp.where(fast, fast_rate, slow_decay_rate)
    rough = jax.random.uniform(keys[3], (HEADS, TOKENS), jnp.float32, 0.5, 1.5)
    starting_index = -rate[:, None] * rough
    places = jax.random.randint(keys[4], (HEADS, 2), 0, TOKENS)
    stack_level = jnp.log(jax.random.uniform(keys[5], (HEADS, 2), jnp.float32, 0.5, 0.8))
    aligned_slot = jnp.arange(TOKENS)[None, None, :] == places[:, :, None]
    spike_span = jnp.sum(jnp.where(aligned_slot, stack_level[:, :, None], 0.0), axis=1)
    return (starting_index + spike_span).astype(jnp.float32)


def spiked(array, rng, source, target, blocks, factor):
    def block_of(dim):
        return (jnp.arange(array.shape[dim]) // (array.shape[dim] // blocks)).reshape((-1,) + (1,) * (array.ndim - 1 - dim))

    near = jax.random.permutation(rng, blocks)[block_of(target)]
    far = (block_of(target) + blocks // 2) % blocks
    return jnp.where((block_of(source) == near) | (block_of(source) == far), factor * array, array)


def shard_levels(key, extent, pieces, smallest, largest):
    loudness = 1.0
    for dim, shards_of in pieces:
        steps = jax.random.uniform(jax.random.fold_in(jax.random.fold_in(key, 6), dim), (shards_of,), jnp.float32, smallest / len(pieces), largest / len(pieces))
        loudness = loudness * jnp.repeat(jnp.exp(steps), extent[dim] // shards_of).reshape((-1,) + (1,) * (len(extent) - 1 - dim))
    return loudness


def normal_values(own_key, dims, width, most, shards=(), kind=jnp.bfloat16):
    drawn = width * jax.random.normal(own_key, dims, jnp.float32)
    if shards:
        drawn = drawn * shard_levels(own_key, dims, shards, -0.22, 0.18)
    return jnp.clip(drawn, -most, most).astype(kind)


def bell_draw_with(stream_key, shape, scale, bound, cuts, heavy, dtype=jnp.bfloat16):
    drawn = scale * jax.random.normal(stream_key, shape, jnp.float32)
    if cuts:
        drawn = drawn * shard_levels(stream_key, shape, cuts, -0.22, 0.18)
    return jnp.clip(spiked(drawn, jax.random.fold_in(stream_key, 3), *heavy), -bound, bound).astype(dtype)


def setup_inputs(seed: int = 0) -> dict:
    seeds = jax.random.split(jax.random.key(seed), 6)
    tokens = normal_values(seeds[0], (TOKENS, D), 1.0, 6.0, ((0, 32),))
    qkv_weight = normal_values(seeds[1], (D, 3, HEADS * HD), D ** -0.5, 0.078125, ((0, 32), (2, 16)))
    out_weight = bell_draw_with(seeds[2], (D, HEADS * HD), (HEADS * HD) ** -0.5, 0.1875, ((0, 32), (1, 16)), (1, 0, 32, 2.75))
    log_decay = draw_log_decay(jax.random.fold_in(seeds[5], 71), 0)
    norm_gain = jnp.clip(1.0 + 0.15 * jax.random.normal(seeds[4], (HEADS * HD,), jnp.float32), 0.25, 1.75)
    return dict(tokens=tokens, qkv_weight=qkv_weight, out_weight=out_weight, log_decay=log_decay, norm_gain=norm_gain)


def reference(tokens, qkv_weight, out_weight, log_decay, norm_gain):
    blocks = TOKENS // TOKENS_PER_SHARD
    group = HEADS * HD // N_DP
    token_blocks = tokens.reshape(blocks, TOKENS_PER_SHARD, D)
    decay_blocks = jnp.transpose(log_decay.reshape(HEADS, blocks, TOKENS_PER_SHARD), (1, 0, 2))
    flat_qkv = qkv_weight.reshape(D, 3 * HEADS * HD)
    out_groups = out_weight.astype(jnp.float32).reshape(D, N_DP, group)
    gain = norm_gain.reshape(HEADS, HD)
    later = jnp.arange(TOKENS_PER_SHARD)[:, None] >= jnp.arange(TOKENS_PER_SHARD)[None, :]

    def step(state, inputs):
        block_tokens, block_decay = inputs
        proj = jnp.dot(block_tokens, flat_qkv, preferred_element_type=jnp.float32)
        proj = proj.reshape(TOKENS_PER_SHARD, 3, HEADS, HD)
        query = jax.nn.silu(proj[:, 0]).astype(jnp.bfloat16).astype(jnp.float32)
        key = jax.nn.silu(proj[:, 1]).astype(jnp.bfloat16).astype(jnp.float32)
        value = proj[:, 2].astype(jnp.bfloat16).astype(jnp.float32)
        cum = jnp.cumsum(block_decay, axis=1)
        scores = jnp.einsum('thd,shd->hts', query, key)
        spread = cum[:, :, None] - cum[:, None, :]
        factor = jnp.where(later[None], jnp.exp(jnp.minimum(spread, 0.0)), 0.0)
        weights = (scores * factor).astype(jnp.bfloat16).astype(jnp.float32)
        intra = jnp.einsum('hts,shd->thd', weights, value)
        lifted = query * jnp.exp(cum).T[:, :, None]
        inter = jnp.einsum('thd,hde->the', lifted, state, precision=lax.Precision.HIGHEST)
        attn = intra + inter
        scaled_key = (key * jnp.exp(cum[:, -1:] - cum).T[:, :, None]).astype(jnp.bfloat16).astype(jnp.float32)
        local = jnp.einsum('thd,the->hde', scaled_key, value)
        new_state = jnp.exp(cum[:, -1])[:, None, None] * state + local
        power = lax.optimization_barrier(jnp.mean(attn * attn, axis=-1, keepdims=True))
        normalized_output = (attn / jnp.sqrt(power + 1e-05) * gain[None]).astype(jnp.bfloat16)
        normalized_output = normalized_output.astype(jnp.float32).reshape(TOKENS_PER_SHARD, N_DP, group)
        partial_value = jnp.einsum('tng,dng->ntd', normalized_output, out_groups)
        partial_value = partial_value.astype(jnp.bfloat16).astype(jnp.float32)
        mixed = lax.optimization_barrier(jnp.sum(partial_value, axis=0)).astype(jnp.bfloat16)
        return (new_state, mixed)
    start = jnp.zeros((HEADS, HD, HD), jnp.float32)
    final_state, outputs = lax.scan(step, start, (token_blocks, decay_blocks))
    return outputs.reshape(TOKENS, D)
```

```python
import jax
import jax.numpy as jnp
from jax import lax
from jax.sharding import PartitionSpec as P


def ring_perm(n, step):
    return [(s, (s + step) % n) for s in range(n)]


def pair_perm(n):
    return [(s, s ^ 1) for s in range(n)]


def exclusive_state(local, log_fall, n):
    heads, hsize, _ = local.shape
    rows = heads * hsize * hsize // (n * 128)
    pieces = local.astype(jnp.bfloat16).reshape(n, rows, 128)
    high = lax.reduce_precision(log_fall, 8, 7)
    middle = lax.reduce_precision(log_fall - high, 8, 7)
    low = lax.reduce_precision(log_fall - high - middle, 8, 7)
    falls = jnp.stack([high, middle, low], axis=1)
    falls = jnp.repeat(falls, n // heads, axis=0).astype(jnp.bfloat16)
    falls = jnp.pad(falls[:, None, :], ((0, 0), (0, rows - 1), (0, 128 - 3)))
    sent = jnp.concatenate([pieces, falls], axis=1)
    got = lax.all_to_all(sent, "seq", 0, 0, tiled=True)
    fall_of = jnp.sum(got[:, rows, :3].astype(jnp.float32), axis=1)
    at = jnp.arange(n)
    between = (at[None, None, :] > at[None, :, None]) & (at[None, None, :] < at[:, None, None])
    total = jnp.sum(jnp.where(between, fall_of[None, None, :], 0.0), axis=2)
    mix = jnp.where(at[None, :] < at[:, None], jnp.exp(total), 0.0)
    slices = got[:, :rows, :].reshape(n, rows * 128).astype(jnp.float32)
    earlier = jnp.dot(mix, slices, precision=lax.Precision.HIGHEST)
    earlier = earlier.astype(jnp.bfloat16).reshape(n, rows, 128)
    back = lax.all_to_all(earlier, "seq", 0, 0, tiled=True)
    return back.reshape(heads, hsize, hsize)


def make_body(n_seq, n_dp):
    n_z = n_seq // 2
    up, down, flip = ring_perm(n_seq, 2), ring_perm(n_seq, -2), pair_perm(n_seq)

    def body(tokens, qkv_weight, out_weight, log_decay, norm_gain):
        rows, depth = tokens.shape
        width = qkv_weight.shape[2]
        heads = log_decay.shape[0]
        hsize = width // heads
        shard = qkv_weight.shape[0]
        place = lax.axis_index("seq")
        z, half = place // 2, place % 2
        core = lax.axis_index("dp") % 2
        f32 = jnp.float32

        parts = jnp.transpose(qkv_weight, (1, 0, 2))
        kv_own = jnp.concatenate([parts[1], parts[2]], axis=1)
        kv_pair = jnp.concatenate([kv_own, lax.ppermute(kv_own, "seq", flip)], axis=0)
        qo_own = jnp.concatenate([parts[0], out_weight], axis=0)

        by_z = jnp.transpose(tokens.reshape(rows, n_z, 2, shard), (1, 0, 2, 3))
        by_z = jnp.concatenate([by_z, by_z[:, :, :1]], axis=2).reshape(n_z, rows, 3, shard)
        tok = lax.dynamic_slice_in_dim(by_z, half, 2, axis=2).reshape(n_z, rows, 2 * shard)

        def tok_of(offset):
            return lax.dynamic_index_in_dim(tok, (z + offset) % n_z, 0, False)

        kv = {0: kv_pair}
        qo_mine = {0: qo_own}
        qo_theirs = {}

        def flip_pieces(offsets):
            joined = jnp.concatenate([qo_mine[o] for o in offsets], axis=0)
            swapped = lax.ppermute(joined, "seq", flip)
            for i, o in enumerate(offsets):
                qo_theirs[o] = swapped[i * 2 * shard : (i + 1) * 2 * shard]

        ahead = behind = jnp.concatenate([kv_pair, qo_own], axis=1)
        flip_pieces([0])
        last = n_z // 2
        for k in range(1, last):
            ahead = lax.ppermute(ahead, "seq", up)
            behind = lax.ppermute(behind, "seq", down)
            kv[-k], kv[k] = ahead[:, : 2 * width], behind[:, : 2 * width]
            qo_mine[-k], qo_mine[k] = ahead[:, 2 * width :], behind[:, 2 * width :]
            flip_pieces([-k, k])
        top = lax.ppermute(ahead[:shard], "seq", up)
        bottom = lax.ppermute(behind[shard:], "seq", down)
        final = jnp.concatenate([top, bottom], axis=0)
        kv[last], qo_mine[last] = final[:, : 2 * width], final[:, 2 * width :]
        flip_pieces([last])

        order = sorted(kv, key=lambda o: (abs(o), o))
        kv_proj = sum(
            jnp.dot(tok_of(o), kv[o], preferred_element_type=f32) for o in order
        )
        q_proj = sum(
            jnp.dot(
                tok_of(o),
                jnp.concatenate([qo_mine[o][:shard], qo_theirs[o][:shard]], axis=0),
                preferred_element_type=f32,
            )
            for o in order
        )
        in_order = list(range(0, n_z // 2 + 1)) + list(range(-(n_z // 2) + 1, 0))
        outs = jnp.stack(
            [jnp.stack([qo_mine[o][shard:], qo_theirs[o][shard:], qo_mine[o][shard:]]) for o in in_order]
        )
        outs = lax.dynamic_slice_in_dim(outs, half, 2, axis=1)
        outs = jnp.roll(outs, z, axis=0).reshape(n_z // 2, 2, 2 * shard, width)
        out_mine = lax.dynamic_index_in_dim(outs, core, 1, False)
        out_theirs = lax.dynamic_index_in_dim(outs, 1 - core, 1, False)

        key = jax.nn.silu(kv_proj[:, :width]).astype(jnp.bfloat16).reshape(rows, heads, hsize)
        value = kv_proj[:, width:].astype(jnp.bfloat16).reshape(rows, heads, hsize)
        query = jax.nn.silu(q_proj).astype(jnp.bfloat16).reshape(rows, heads, hsize)
        cum = jnp.cumsum(log_decay, axis=1)
        scaled_key = (key.astype(f32) * jnp.exp(cum[:, -1:] - cum).T[:, :, None]).astype(jnp.bfloat16)
        local = jnp.einsum("thd,the->hde", scaled_key, value, preferred_element_type=f32)
        earlier_state = exclusive_state(local, cum[:, -1], n_seq)

        later = jnp.arange(rows)[:, None] >= jnp.arange(rows)[None, :]
        scores = jnp.einsum("thd,shd->hts", query, key, preferred_element_type=f32)
        spread = cum[:, :, None] - cum[:, None, :]
        factor = jnp.where(later[None], jnp.exp(jnp.minimum(spread, 0.0)), 0.0)
        weights = (scores * factor).astype(jnp.bfloat16)
        intra = jnp.einsum("hts,shd->thd", weights, value, preferred_element_type=f32)
        carried = jnp.einsum("thd,hde->the", query, earlier_state, preferred_element_type=f32)
        attn = intra + carried * jnp.exp(cum).T[:, :, None]
        power = jnp.mean(attn * attn, axis=-1, keepdims=True)
        gain = norm_gain.reshape(heads, hsize)
        normed = (attn / jnp.sqrt(power + 1e-05) * gain[None]).astype(jnp.bfloat16).reshape(rows, width)

        wide = jnp.broadcast_to(normed[None], (n_dp // 2, rows, width))
        give = jnp.einsum("itg,idg->itd", wide, out_theirs, preferred_element_type=f32)
        taken = lax.ppermute(give.astype(jnp.bfloat16), "dp", pair_perm(n_dp))
        keep = jnp.einsum("itg,idg->itd", wide, out_mine, preferred_element_type=f32)
        keep = keep.astype(jnp.bfloat16).astype(f32) + taken.astype(f32)
        groups = [[2 * i + c for i in range(n_dp // 2)] for c in range(2)]
        spread_out = lax.all_to_all(keep.astype(jnp.bfloat16), "dp", 0, 0, axis_index_groups=groups, tiled=True)
        return jnp.sum(spread_out.astype(f32), axis=0).astype(jnp.bfloat16)

    return body


def solution(mesh):
    body = make_body(mesh.shape["seq"], mesh.shape["dp"])
    in_specs = (P("seq", None), P("seq", None, "dp"), P("seq", "dp"), P("dp", "seq"), P("dp"))
    return jax.shard_map(body, mesh=mesh, in_specs=in_specs, out_specs=P("seq", "dp"), check_vma=False)
```

```python
import jax
import jax.numpy as jnp
from jax import lax
from jax.sharding import PartitionSpec as P


def ring_perm(n, step):
    return [(s, (s + step) % n) for s in range(n)]


def pair_perm(n):
    return [(s, s ^ 1) for s in range(n)]


def three_parts(x):
    high = lax.reduce_precision(x, 8, 7)
    middle = lax.reduce_precision(x - high, 8, 7)
    return jnp.stack([high, middle, x - high - middle], axis=-1).astype(jnp.bfloat16)


def exclusive_state(local, log_fall, half, n):
    f32 = jnp.float32
    heads, hsize, _ = local.shape
    n_z = n // 2
    rows = heads * hsize * hsize // (n_z * 128)
    flat = local.astype(jnp.bfloat16).reshape(heads * hsize, hsize)
    tail = jnp.pad(three_parts(log_fall), ((0, 16 - heads), (0, hsize - 3)))
    got = lax.ppermute(jnp.concatenate([flat, tail], axis=0), "seq", pair_perm(n))
    other = got[: heads * hsize].astype(f32).reshape(heads, hsize, hsize)
    other_fall = jnp.sum(got[heads * hsize : heads * hsize + heads, :3].astype(f32), axis=1)
    joined = jnp.where(
        half == 0,
        jnp.exp(other_fall)[:, None, None] * local + other,
        jnp.exp(log_fall)[:, None, None] * other + local,
    )
    slices = joined.astype(jnp.bfloat16).reshape(n_z, rows, 128)
    falls = jnp.repeat(three_parts(log_fall + other_fall), n_z // heads, axis=0)
    falls = jnp.pad(falls[:, None, :], ((0, 0), (0, 7), (0, 128 - 3)))
    groups = [[2 * i + x for i in range(n_z)] for x in range(2)]
    sent = jnp.concatenate([slices, falls], axis=1)
    got = lax.all_to_all(sent, "seq", 0, 0, axis_index_groups=groups, tiled=True)
    fall_of = jnp.sum(got[:, rows, :3].astype(f32), axis=1)
    at = jnp.arange(n_z)
    between = (at[None, None, :] > at[None, :, None]) & (at[None, None, :] < at[:, None, None])
    total = jnp.sum(jnp.where(between, fall_of[None, None, :], 0.0), axis=2)
    mix = jnp.where(at[None, :] < at[:, None], jnp.exp(total), 0.0)
    slices = got[:, :rows, :].reshape(n_z, rows * 128).astype(f32)
    earlier = jnp.dot(mix, slices, precision=lax.Precision.HIGHEST)
    earlier = earlier.astype(jnp.bfloat16).reshape(n_z, rows, 128)
    back = lax.all_to_all(earlier, "seq", 0, 0, axis_index_groups=groups, tiled=True)
    back = back.reshape(heads, hsize, hsize)
    after = jnp.exp(other_fall)[:, None, None] * back.astype(f32) + other
    return jnp.where(half == 0, back, after.astype(jnp.bfloat16))


def make_body(n_seq, n_dp):
    n_z = n_seq // 2
    up, down, flip = ring_perm(n_seq, 2), ring_perm(n_seq, -2), pair_perm(n_seq)

    def layer(tokens, qkv_weight, out_weight, log_decay, norm_gain):
        rows, _ = tokens.shape
        width = qkv_weight.shape[2]
        heads = log_decay.shape[0]
        hsize = width // heads
        shard = qkv_weight.shape[0]
        place = lax.axis_index("seq")
        z, half = place // 2, place % 2
        core = lax.axis_index("dp") % 2
        f32 = jnp.float32

        parts = jnp.transpose(qkv_weight, (1, 0, 2))
        own = jnp.concatenate([parts[1], parts[2], parts[0], out_weight], axis=1)
        pieces = {0: own}
        last = n_z // 2
        ahead = behind = own
        for k in range(1, last):
            ahead = lax.ppermute(ahead, "seq", up)
            behind = lax.ppermute(behind, "seq", down)
            pieces[-k], pieces[k] = ahead, behind
        top = lax.ppermute(ahead[: shard // 2], "seq", up)
        bottom = lax.ppermute(behind[shard // 2 :], "seq", down)
        pieces[last] = jnp.concatenate([top, bottom], axis=0)
        order = sorted(pieces, key=lambda o: (abs(o), o))

        by_z = tokens.T.reshape(n_z, 2, shard, rows)
        mine = lax.dynamic_index_in_dim(by_z, half, 1, False)
        theirs = lax.dynamic_index_in_dim(by_z, 1 - half, 1, False)
        theirs = lax.ppermute(theirs, "seq", flip)
        both = jnp.concatenate([mine, theirs], axis=2)

        def times(o):
            tok = lax.dynamic_index_in_dim(both, (z + o) % n_z, 0, False)
            weight = pieces[o][:, : 3 * width]
            return lax.dot_general(tok, weight, (((0,), (0,)), ((), ())), preferred_element_type=f32)

        def combine(partial):
            sent = lax.ppermute(partial[rows:].astype(jnp.bfloat16), "seq", flip)
            return partial[:rows] + sent.astype(f32)

        proj = sum(times(o) for o in order)
        kv_proj = combine(proj[:, : 2 * width])
        q_proj = combine(proj[:, 2 * width :])

        other_outs = {}
        for batch in (order[:7], order[7:13], order[13:]):
            joined = jnp.concatenate([pieces[o][:, 3 * width :] for o in batch], axis=0)
            swapped = lax.ppermute(joined, "seq", flip)
            for i, o in enumerate(batch):
                other_outs[o] = swapped[i * shard : (i + 1) * shard]
        in_order = list(range(0, last + 1)) + list(range(-last + 1, 0))
        outs = jnp.stack(
            [
                jnp.stack([pieces[o][:, 3 * width :], other_outs[o], pieces[o][:, 3 * width :]])
                for o in in_order
            ]
        )
        outs = lax.dynamic_slice_in_dim(outs, half, 2, axis=1)
        outs = jnp.roll(outs, z, axis=0).reshape(n_z // 2, 2, 2 * shard, width)
        out_mine = lax.dynamic_index_in_dim(outs, core, 1, False)
        out_theirs = lax.dynamic_index_in_dim(outs, 1 - core, 1, False)

        key = jax.nn.silu(kv_proj[:, :width]).astype(jnp.bfloat16).reshape(rows, heads, hsize)
        value = kv_proj[:, width:].astype(jnp.bfloat16).reshape(rows, heads, hsize)
        query = jax.nn.silu(q_proj).astype(jnp.bfloat16).reshape(rows, heads, hsize)
        cum = jnp.cumsum(log_decay, axis=1)
        scaled_key = (key.astype(f32) * jnp.exp(cum[:, -1:] - cum).T[:, :, None]).astype(jnp.bfloat16)
        local = jnp.einsum("thd,the->hde", scaled_key, value, preferred_element_type=f32)
        earlier_state = exclusive_state(local, cum[:, -1], half, n_seq)

        later = jnp.arange(rows)[:, None] >= jnp.arange(rows)[None, :]
        scores = jnp.einsum("thd,shd->hts", query, key, preferred_element_type=f32)
        spread = cum[:, :, None] - cum[:, None, :]
        factor = jnp.where(later[None], jnp.exp(jnp.minimum(spread, 0.0)), 0.0)
        weights = (scores * factor).astype(jnp.bfloat16)
        intra = jnp.einsum("hts,shd->thd", weights, value, preferred_element_type=f32)
        carried = jnp.einsum("thd,hde->the", query, earlier_state, preferred_element_type=f32)
        attn = intra + carried * jnp.exp(cum).T[:, :, None]
        power = jnp.mean(attn * attn, axis=-1, keepdims=True)
        gain = norm_gain.reshape(heads, hsize)
        normed = (attn / jnp.sqrt(power + 1e-05) * gain[None]).astype(jnp.bfloat16).reshape(rows, width)

        wide = jnp.broadcast_to(normed[None], (n_dp // 2, rows, width))
        give = jnp.einsum("itg,idg->itd", wide, out_theirs, preferred_element_type=f32)
        taken = lax.ppermute(give.astype(jnp.bfloat16), "dp", pair_perm(n_dp))
        keep = jnp.einsum("itg,idg->itd", wide, out_mine, preferred_element_type=f32)
        keep = keep.astype(jnp.bfloat16).astype(f32) + taken.astype(f32)
        groups = [[2 * i + c for i in range(n_dp // 2)] for c in range(2)]
        spread_out = lax.all_to_all(keep.astype(jnp.bfloat16), "dp", 0, 0, axis_index_groups=groups, tiled=True)
        return jnp.sum(spread_out.astype(f32), axis=0).astype(jnp.bfloat16)

    return layer


def solution(mesh):
    body = make_body(mesh.shape["seq"], mesh.shape["dp"])
    in_specs = (P("seq", None), P("seq", None, "dp"), P("seq", "dp"), P("dp", "seq"), P("dp"))
    return jax.shard_map(body, mesh=mesh, in_specs=in_specs, out_specs=P("seq", "dp"), check_vma=False)
```

```python
import jax
import jax.numpy as jnp
from jax import lax
from jax.sharding import PartitionSpec as P


def ring_perm(n, step):
    return [(s, (s + step) % n) for s in range(n)]


def pair_perm(n):
    return [(s, s ^ 1) for s in range(n)]


def exclusive_state(local, log_fall, n):
    heads, hsize, _ = local.shape
    rows = heads * hsize * hsize // (n * 128)
    pieces = local.astype(jnp.bfloat16).reshape(n, rows, 128)
    high = lax.reduce_precision(log_fall, 8, 7)
    middle = lax.reduce_precision(log_fall - high, 8, 7)
    low = lax.reduce_precision(log_fall - high - middle, 8, 7)
    falls = jnp.stack([high, middle, low], axis=1)
    falls = jnp.repeat(falls, n // heads, axis=0).astype(jnp.bfloat16)
    falls = jnp.pad(falls[:, None, :], ((0, 0), (0, rows - 1), (0, 128 - 3)))
    sent = jnp.concatenate([pieces, falls], axis=1)
    got = lax.all_to_all(sent, "seq", 0, 0, tiled=True)
    fall_of = jnp.sum(got[:, rows, :3].astype(jnp.float32), axis=1)
    at = jnp.arange(n)
    between = (at[None, None, :] > at[None, :, None]) & (at[None, None, :] < at[:, None, None])
    total = jnp.sum(jnp.where(between, fall_of[None, None, :], 0.0), axis=2)
    mix = jnp.where(at[None, :] < at[:, None], jnp.exp(total), 0.0)
    slices = got[:, :rows, :].reshape(n, rows * 128).astype(jnp.float32)
    earlier = jnp.dot(mix, slices, precision=lax.Precision.HIGHEST)
    earlier = earlier.astype(jnp.bfloat16).reshape(n, rows, 128)
    back = lax.all_to_all(earlier, "seq", 0, 0, tiled=True)
    return back.reshape(heads, hsize, hsize)


def make_body(n_seq, n_dp):
    n_z = n_seq // 2
    up, down, flip = ring_perm(n_seq, 2), ring_perm(n_seq, -2), pair_perm(n_seq)

    def layer(tokens, qkv_weight, out_weight, log_decay, norm_gain):
        rows, _ = tokens.shape
        width = qkv_weight.shape[2]
        heads = log_decay.shape[0]
        hsize = width // heads
        shard = qkv_weight.shape[0]
        place = lax.axis_index("seq")
        z, half = place // 2, place % 2
        core = lax.axis_index("dp") % 2
        f32 = jnp.float32

        parts = jnp.transpose(qkv_weight, (1, 0, 2))
        own = jnp.concatenate([parts[1], parts[2], parts[0], out_weight], axis=1)
        pieces = {0: own}
        last = n_z // 2
        ahead = behind = own
        for k in range(1, last):
            ahead = lax.ppermute(ahead, "seq", up)
            behind = lax.ppermute(behind, "seq", down)
            pieces[-k], pieces[k] = ahead, behind
        top = lax.ppermute(ahead[: shard // 2], "seq", up)
        bottom = lax.ppermute(behind[shard // 2 :], "seq", down)
        pieces[last] = jnp.concatenate([top, bottom], axis=0)

        by_z = tokens.T.reshape(n_z, 2, shard, rows)
        by_z, _ = lax.optimization_barrier((by_z, pieces[-1]))
        by_z = jnp.concatenate([by_z, by_z], axis=0)
        by_z = lax.dynamic_slice_in_dim(by_z, (z + last) % n_z, n_z, axis=0)
        mine = lax.dynamic_index_in_dim(by_z, half, 1, False)
        theirs = lax.dynamic_index_in_dim(by_z, 1 - half, 1, False)
        theirs = lax.ppermute(theirs, "seq", flip)

        inner, outer = last // 2, last - 2
        groups = [
            list(range(-inner, inner + 1)),
            list(range(-outer, -inner)) + list(range(inner + 1, outer + 1)),
            [1 - last, last - 1, last],
        ]

        def times(toks, weight, group):
            tok = jnp.concatenate([toks[(o + last) % n_z] for o in group], axis=0)
            return lax.dot_general(tok, weight, (((0,), (0,)), ((), ())), preferred_element_type=f32)

        def join(partial, keep):
            sent = lax.ppermute(partial.astype(jnp.bfloat16), "seq", flip)
            return keep + sent.astype(f32)

        columns = 3 * width
        mine_sum = theirs_sum = None
        for group in groups[:2]:
            weight = jnp.concatenate([pieces[o][:, :columns] for o in group], axis=0)
            part = times(mine, weight, group)
            mine_sum = part if mine_sum is None else mine_sum + part
            part = times(theirs, weight, group)
            theirs_sum = part if theirs_sum is None else theirs_sum + part
        final = jnp.concatenate([pieces[o] for o in groups[2]], axis=0)
        kv_cols, q_cols = slice(0, 2 * width), slice(2 * width, columns)
        away = theirs_sum[:, kv_cols] + times(theirs, final[:, kv_cols], groups[2])
        kv_proj = join(away, mine_sum[:, kv_cols] + times(mine, final[:, kv_cols], groups[2]))
        away = theirs_sum[:, q_cols] + times(theirs, final[:, q_cols], groups[2])
        q_proj = join(away, mine_sum[:, q_cols] + times(mine, final[:, q_cols], groups[2]))

        other_outs = {}
        for batch in groups:
            joined = jnp.concatenate([pieces[o][:, 3 * width :] for o in batch], axis=0)
            swapped = lax.ppermute(joined, "seq", flip)
            for i, o in enumerate(batch):
                other_outs[o] = swapped[i * shard : (i + 1) * shard]
        key = jax.nn.silu(kv_proj[:, :width]).astype(jnp.bfloat16).reshape(rows, heads, hsize)
        value = kv_proj[:, width:].astype(jnp.bfloat16).reshape(rows, heads, hsize)
        query = jax.nn.silu(q_proj).astype(jnp.bfloat16).reshape(rows, heads, hsize)
        cum = jnp.cumsum(log_decay, axis=1)
        scaled_key = (key.astype(f32) * jnp.exp(cum[:, -1:] - cum).T[:, :, None]).astype(jnp.bfloat16)
        local = jnp.einsum("thd,the->hde", scaled_key, value, preferred_element_type=f32)
        in_order = list(range(0, last + 1)) + list(range(-last + 1, 0))
        own_outs = {o: pieces[o][:, 3 * width :] for o in in_order}
        (own_outs, other_outs), _ = lax.optimization_barrier(((own_outs, other_outs), local))
        outs = jnp.stack(
            [
                jnp.stack([own_outs[o], other_outs[o], own_outs[o]])
                for o in in_order
            ]
        )
        outs = lax.dynamic_slice_in_dim(outs, half, 2, axis=1)
        outs = jnp.roll(outs, z, axis=0).reshape(n_z // 2, 2, 2 * shard, width)
        out_mine = lax.dynamic_index_in_dim(outs, core, 1, False)
        out_theirs = lax.dynamic_index_in_dim(outs, 1 - core, 1, False)

        earlier_state = exclusive_state(local, cum[:, -1], n_seq)

        later = jnp.arange(rows)[:, None] >= jnp.arange(rows)[None, :]
        scores = jnp.einsum("thd,shd->hts", query, key, preferred_element_type=f32)
        spread = cum[:, :, None] - cum[:, None, :]
        factor = jnp.where(later[None], jnp.exp(jnp.minimum(spread, 0.0)), 0.0)
        weights = (scores * factor).astype(jnp.bfloat16)
        intra = jnp.einsum("hts,shd->thd", weights, value, preferred_element_type=f32)
        intra = lax.optimization_barrier(intra)
        carried = jnp.einsum("thd,hde->the", query, earlier_state, preferred_element_type=f32)
        attn = intra + carried * jnp.exp(cum).T[:, :, None]
        power = jnp.mean(attn * attn, axis=-1, keepdims=True)
        gain = norm_gain.reshape(heads, hsize)
        normed = (attn / jnp.sqrt(power + 1e-05) * gain[None]).astype(jnp.bfloat16).reshape(rows, width)

        wide = jnp.broadcast_to(normed[None], (n_dp // 2, rows, width))
        give = jnp.einsum("itg,idg->itd", wide, out_theirs, preferred_element_type=f32)
        taken = lax.ppermute(give.astype(jnp.bfloat16), "dp", pair_perm(n_dp))
        keep = jnp.einsum("itg,idg->itd", wide, out_mine, preferred_element_type=f32)
        keep = keep.astype(jnp.bfloat16).astype(f32) + taken.astype(f32)
        groups = [[2 * i + c for i in range(n_dp // 2)] for c in range(2)]
        spread_out = lax.all_to_all(keep.astype(jnp.bfloat16), "dp", 0, 0, axis_index_groups=groups, tiled=True)
        return jnp.sum(spread_out.astype(f32), axis=0).astype(jnp.bfloat16)

    return layer


def solution(mesh):
    body = make_body(mesh.shape["seq"], mesh.shape["dp"])
    in_specs = (P("seq", None), P("seq", None, "dp"), P("seq", "dp"), P("dp", "seq"), P("dp"))
    return jax.shard_map(body, mesh=mesh, in_specs=in_specs, out_specs=P("seq", "dp"), check_vma=False)
```

```python
import jax
import jax.numpy as jnp
from jax import lax
from jax.sharding import PartitionSpec as P
from jax.experimental import pallas as pl
from jax.experimental.pallas import tpu as pltpu


def ring_perm(n, step):
    return [(s, (s + step) % n) for s in range(n)]


def pair_perm(n):
    return [(s, s ^ 1) for s in range(n)]


def exclusive_state(local, log_fall, n, where):
    heads, hsize, _ = local.shape
    rows = heads * hsize * hsize // (n * 128)
    pieces = local.astype(jnp.bfloat16).reshape(n, rows, 128)
    high = lax.reduce_precision(log_fall, 8, 7)
    middle = lax.reduce_precision(log_fall - high, 8, 7)
    low = lax.reduce_precision(log_fall - high - middle, 8, 7)
    falls = jnp.stack([high, middle, low], axis=1)
    falls = jnp.repeat(falls, n // heads, axis=0).astype(jnp.bfloat16)
    falls = jnp.pad(falls[:, None, :], ((0, 0), (0, rows - 1), (0, 128 - 3)))
    sent = jnp.concatenate([pieces, falls], axis=1)
    got = lax.all_to_all(sent, "seq", 0, 0, tiled=True)
    fall_of = jnp.sum(got[:, rows, :3].astype(jnp.float32), axis=1)
    at = jnp.arange(n)
    between = (at[None, None, :] > at[None, :, None]) & (at[None, None, :] < at[:, None, None])
    total = jnp.sum(jnp.where(between, fall_of[None, None, :], 0.0), axis=2)
    mix = jnp.where(at[None, :] < at[:, None], jnp.exp(total), 0.0)
    slices = got[:, :rows, :].reshape(n, rows * 128).astype(jnp.float32)
    earlier = jnp.dot(mix, slices, precision=lax.Precision.HIGHEST)
    earlier = earlier.astype(jnp.bfloat16).reshape(n, rows, 128)
    earlier, where = lax.optimization_barrier((earlier, where))
    back = lax.all_to_all(earlier, "seq", 0, 0, tiled=True)
    return back.reshape(heads, hsize, hsize), where


def place_outs(where, blocks, n_z, shard, width):
    def kernel(where_ref, *refs):
        sources, out, sems = refs[: len(set_of)], refs[len(set_of)], refs[len(set_of) + 1]
        z, half, core = where_ref[0], where_ref[1], where_ref[2]
        copies = []
        for n, (source, row, column, offset, other) in enumerate(items):
            at = lax.rem(z + (offset + n_z), n_z)
            chip, part = lax.div(at, 2), lax.rem(at, 2)
            away = lax.rem(part + core, 2)
            side = half if other == 0 else 1 - half
            copies.append(
                pltpu.make_async_copy(
                    sources[source].at[pl.ds(row, shard), pl.ds(column, width)],
                    out.at[away, chip, pl.ds(side * shard, shard), :],
                    sems.at[n],
                )
            )
        for copy in copies:
            copy.start()
        for copy in copies:
            copy.wait()

    set_of, items = [], []
    for array, row, column, offset, other in blocks:
        known = [i for i, a in enumerate(set_of) if a is array]
        if not known:
            set_of.append(array)
        items.append((known[0] if known else len(set_of) - 1, row, column, offset, other))
    return pl.pallas_call(
        kernel,
        out_shape=jax.ShapeDtypeStruct((2, n_z // 2, 2 * shard, width), jnp.bfloat16),
        in_specs=[pl.BlockSpec(memory_space=pltpu.SMEM)] + [pl.BlockSpec(memory_space=pl.ANY)] * len(set_of),
        out_specs=pl.BlockSpec(memory_space=pl.ANY),
        scratch_shapes=[pltpu.SemaphoreType.DMA((len(items),))],
        name="place_outs",
    )(where, *set_of)


def make_body(n_seq, n_dp):
    n_z = n_seq // 2
    up, down, flip = ring_perm(n_seq, 2), ring_perm(n_seq, -2), pair_perm(n_seq)

    def layer(tokens, qkv_weight, out_weight, log_decay, norm_gain):
        rows, _ = tokens.shape
        width = qkv_weight.shape[2]
        heads = log_decay.shape[0]
        hsize = width // heads
        shard = qkv_weight.shape[0]
        place = lax.axis_index("seq")
        z, half = place // 2, place % 2
        core = lax.axis_index("dp") % 2
        f32 = jnp.float32

        parts = jnp.transpose(qkv_weight, (1, 0, 2))
        own = jnp.concatenate([parts[1], parts[2], parts[0], out_weight], axis=1)
        pieces = {0: own}
        last = n_z // 2
        ahead = behind = own
        for k in range(1, last):
            ahead = lax.ppermute(ahead, "seq", up)
            behind = lax.ppermute(behind, "seq", down)
            pieces[-k], pieces[k] = ahead, behind
        top = lax.ppermute(ahead[: shard // 2], "seq", up)
        bottom = lax.ppermute(behind[shard // 2 :], "seq", down)
        pieces[last] = jnp.concatenate([top, bottom], axis=0)

        by_z = tokens.T.reshape(n_z, 2, shard, rows)
        by_z, _ = lax.optimization_barrier((by_z, pieces[-1]))
        by_z = jnp.concatenate([by_z, by_z], axis=0)
        by_z = lax.dynamic_slice_in_dim(by_z, (z + last) % n_z, n_z, axis=0)
        mine = lax.dynamic_index_in_dim(by_z, half, 1, False)
        theirs = lax.dynamic_index_in_dim(by_z, 1 - half, 1, False)
        theirs = lax.ppermute(theirs, "seq", flip)

        inner, outer = last // 2, last - 2
        groups = [
            list(range(-inner, inner + 1)),
            list(range(-outer, -inner)) + list(range(inner + 1, outer + 1)),
            [1 - last, last - 1, last],
        ]

        def times(toks, weight, group):
            if group == groups[0]:
                tok = toks[last - inner : last + inner + 1].reshape(len(group) * shard, rows)
            else:
                tok = jnp.concatenate([toks[(o + last) % n_z] for o in group], axis=0)
            return lax.dot_general(tok, weight, (((0,), (0,)), ((), ())), preferred_element_type=f32)

        def join(partial, keep):
            sent = lax.ppermute(partial.astype(jnp.bfloat16), "seq", flip)
            return keep + sent.astype(f32)

        columns = 3 * width
        mine_sum = theirs_sum = None
        for group in groups[:2]:
            weight = jnp.concatenate([pieces[o][:, :columns] for o in group], axis=0)
            part = times(mine, weight, group)
            mine_sum = part if mine_sum is None else mine_sum + part
            part = times(theirs, weight, group)
            theirs_sum = part if theirs_sum is None else theirs_sum + part
        final = jnp.concatenate([pieces[o] for o in groups[2]], axis=0)
        kv_cols, q_cols = slice(0, 2 * width), slice(2 * width, columns)
        away = theirs_sum[:, kv_cols] + times(theirs, final[:, kv_cols], groups[2])
        kv_proj = join(away, mine_sum[:, kv_cols] + times(mine, final[:, kv_cols], groups[2]))
        away = theirs_sum[:, q_cols] + times(theirs, final[:, q_cols], groups[2])
        q_proj = join(away, mine_sum[:, q_cols] + times(mine, final[:, q_cols], groups[2]))

        blocks = []
        for batch in groups:
            joined = jnp.concatenate([pieces[o][:, 3 * width :] for o in batch], axis=0)
            swapped = lax.ppermute(joined, "seq", flip)
            blocks += [(swapped, i * shard, 0, o, 1) for i, o in enumerate(batch)]
            blocks += [(pieces[o], 0, 3 * width, o, 0) for o in batch]

        key = jax.nn.silu(kv_proj[:, :width]).astype(jnp.bfloat16).reshape(rows, heads, hsize)
        value = kv_proj[:, width:].astype(jnp.bfloat16).reshape(rows, heads, hsize)
        query = jax.nn.silu(q_proj).astype(jnp.bfloat16).reshape(rows, heads, hsize)
        cum = jnp.cumsum(log_decay, axis=1)
        scaled_key = (key.astype(f32) * jnp.exp(cum[:, -1:] - cum).T[:, :, None]).astype(jnp.bfloat16)
        local = jnp.einsum("thd,the->hde", scaled_key, value, preferred_element_type=f32)
        where = jnp.stack([z, half, core]).astype(jnp.int32)
        earlier_state, where = exclusive_state(local, cum[:, -1], n_seq, where)
        outs = place_outs(where, blocks, n_z, shard, width)
        out_mine, out_theirs = outs[0], outs[1]

        later = jnp.arange(rows)[:, None] >= jnp.arange(rows)[None, :]
        scores = jnp.einsum("thd,shd->hts", query, key, preferred_element_type=f32)
        spread = cum[:, :, None] - cum[:, None, :]
        factor = jnp.where(later[None], jnp.exp(jnp.minimum(spread, 0.0)), 0.0)
        weights = (scores * factor).astype(jnp.bfloat16)
        intra = jnp.einsum("hts,shd->thd", weights, value, preferred_element_type=f32)
        intra = lax.optimization_barrier(intra)
        carried = jnp.einsum("thd,hde->the", query, earlier_state, preferred_element_type=f32)
        attn = intra + carried * jnp.exp(cum).T[:, :, None]
        power = jnp.mean(attn * attn, axis=-1, keepdims=True)
        gain = norm_gain.reshape(heads, hsize)
        normed = (attn / jnp.sqrt(power + 1e-05) * gain[None]).astype(jnp.bfloat16).reshape(rows, width)

        wide = jnp.broadcast_to(normed[None], (n_dp // 2, rows, width))
        give = jnp.einsum("itg,idg->itd", wide, out_theirs, preferred_element_type=f32)
        taken = lax.ppermute(give.astype(jnp.bfloat16), "dp", pair_perm(n_dp))
        keep = jnp.einsum("itg,idg->itd", wide, out_mine, preferred_element_type=f32)
        keep = lax.optimization_barrier(keep.astype(jnp.bfloat16)).astype(f32) + taken.astype(f32)
        groups = [[2 * i + c for i in range(n_dp // 2)] for c in range(2)]
        spread_out = lax.all_to_all(keep.astype(jnp.bfloat16), "dp", 0, 0, axis_index_groups=groups, tiled=True)
        return jnp.sum(spread_out.astype(f32), axis=0).astype(jnp.bfloat16)

    return layer


def solution(mesh):
    body = make_body(mesh.shape["seq"], mesh.shape["dp"])
    in_specs = (P("seq", None), P("seq", None, "dp"), P("seq", "dp"), P("dp", "seq"), P("dp"))
    return jax.shard_map(body, mesh=mesh, in_specs=in_specs, out_specs=P("seq", "dp"), check_vma=False)
```

```python
import jax
import jax.numpy as jnp
from jax import lax
from jax.sharding import PartitionSpec as P
from jax.experimental import pallas as pl
from jax.experimental.pallas import tpu as pltpu


def ring_perm(n, step):
    return [(s, (s + step) % n) for s in range(n)]


def pair_perm(n):
    return [(s, s ^ 1) for s in range(n)]


def exclusive_state(local, log_fall, n, where):
    heads, hsize, _ = local.shape
    rows = heads * hsize * hsize // (n * 128)
    pieces = local.astype(jnp.bfloat16).reshape(n, rows, 128)
    high = lax.reduce_precision(log_fall, 8, 7)
    middle = lax.reduce_precision(log_fall - high, 8, 7)
    low = lax.reduce_precision(log_fall - high - middle, 8, 7)
    falls = jnp.stack([high, middle, low], axis=1)
    falls = jnp.repeat(falls, n // heads, axis=0).astype(jnp.bfloat16)
    falls = jnp.pad(falls[:, None, :], ((0, 0), (0, rows - 1), (0, 128 - 3)))
    sent = jnp.concatenate([pieces, falls], axis=1)
    got = lax.all_to_all(sent, "seq", 0, 0, tiled=True)
    fall_of = jnp.sum(got[:, rows, :3].astype(jnp.float32), axis=1)
    at = jnp.arange(n)
    between = (at[None, None, :] > at[None, :, None]) & (at[None, None, :] < at[:, None, None])
    total = jnp.sum(jnp.where(between, fall_of[None, None, :], 0.0), axis=2)
    mix = jnp.where(at[None, :] < at[:, None], jnp.exp(total), 0.0)
    slices = got[:, :rows, :].reshape(n, rows * 128).astype(jnp.float32)
    earlier = jnp.dot(mix, slices, precision=lax.Precision.HIGHEST)
    earlier = earlier.astype(jnp.bfloat16).reshape(n, rows, 128)
    earlier, where = lax.optimization_barrier((earlier, where))
    back = lax.all_to_all(earlier, "seq", 0, 0, tiled=True)
    return back.reshape(heads, hsize, hsize), where


def whole(shape):
    return pl.BlockSpec(shape, lambda i: (0,) * len(shape), pipeline_mode=pl.Buffered(1))


def place_outs(where, own, own_at, swapped, swapped_at, n_z, shard, width):
    def kernel(where_ref, *refs):
        out = refs[-1]
        z, half, core = where_ref[0], where_ref[1], where_ref[2]

        def place(block, offset, side):
            at = lax.rem(z + (offset + n_z), n_z)
            away = lax.rem(lax.rem(at, 2) + core, 2)
            rows = pl.ds(pl.multiple_of(side * shard, shard), shard)
            out[away, lax.div(at, 2), rows, :] = block

        for ref, offset in zip(refs, own_at):
            place(ref[...], offset, half)
        for ref, offsets in zip(refs[len(own) :], swapped_at):
            for n, offset in enumerate(offsets):
                place(ref[n * shard : (n + 1) * shard, :], offset, 1 - half)

    shape = (2, n_z // 2, 2 * shard, width)
    return pl.pallas_call(
        kernel,
        out_shape=jax.ShapeDtypeStruct(shape, jnp.bfloat16),
        grid=(1,),
        in_specs=[pl.BlockSpec(memory_space=pltpu.SMEM)]
        + [pl.BlockSpec((shard, width), lambda i: (0, 3), pipeline_mode=pl.Buffered(1))] * len(own)
        + [whole(a.shape) for a in swapped],
        out_specs=whole(shape),
        compiler_params=pltpu.CompilerParams(vmem_limit_bytes=24 << 20),
        name="place_outs",
    )(where, *own, *swapped)


def project(mine, theirs, sums, pieces, places, width):
    def kernel(mine_ref, theirs_ref, *refs):
        weights, outs = refs[len(sums) : len(sums) + len(pieces)], refs[-2:]
        for n, (tok, out) in enumerate(zip((mine_ref, theirs_ref), outs)):
            total = refs[n][...] if sums else None
            for weight, place in zip(weights, places):
                part = lax.dot_general(
                    tok[place], weight[...], (((0,), (0,)), ((), ())), preferred_element_type=jnp.float32
                )
                total = part if total is None else total + part
            out[...] = total

    shard = pieces[0].shape[0]
    shape = (mine.shape[2], 3 * width)
    return pl.pallas_call(
        kernel,
        out_shape=[jax.ShapeDtypeStruct(shape, jnp.float32)] * 2,
        grid=(1,),
        in_specs=[whole(mine.shape)] * 2
        + [whole(shape)] * len(sums)
        + [pl.BlockSpec((shard, 3 * width), lambda i: (0, 0), pipeline_mode=pl.Buffered(1))] * len(pieces),
        out_specs=[whole(shape)] * 2,
        compiler_params=pltpu.CompilerParams(vmem_limit_bytes=32 << 20),
        name="project",
    )(mine, theirs, *sums, *pieces)


def make_body(n_seq, n_dp):
    n_z = n_seq // 2
    up, down, flip = ring_perm(n_seq, 2), ring_perm(n_seq, -2), pair_perm(n_seq)

    def layer(tokens, qkv_weight, out_weight, log_decay, norm_gain):
        rows, _ = tokens.shape
        width = qkv_weight.shape[2]
        heads = log_decay.shape[0]
        hsize = width // heads
        shard = qkv_weight.shape[0]
        place = lax.axis_index("seq")
        z, half = place // 2, place % 2
        core = lax.axis_index("dp") % 2
        f32 = jnp.float32

        parts = jnp.transpose(qkv_weight, (1, 0, 2))
        own = jnp.concatenate([parts[1], parts[2], parts[0], out_weight], axis=1)
        pieces = {0: own}
        last = n_z // 2
        ahead = behind = own
        for k in range(1, last):
            ahead = lax.ppermute(ahead, "seq", up)
            behind = lax.ppermute(behind, "seq", down)
            pieces[-k], pieces[k] = ahead, behind
        top = lax.ppermute(ahead[: shard // 2], "seq", up)
        bottom = lax.ppermute(behind[shard // 2 :], "seq", down)
        pieces[last] = jnp.concatenate([top, bottom], axis=0)

        by_z = tokens.T.reshape(n_z, 2, shard, rows)
        by_z, _ = lax.optimization_barrier((by_z, pieces[-1]))
        by_z = jnp.concatenate([by_z, by_z], axis=0)
        by_z = lax.dynamic_slice_in_dim(by_z, (z + last) % n_z, n_z, axis=0)
        mine = lax.dynamic_index_in_dim(by_z, half, 1, False)
        theirs = lax.dynamic_index_in_dim(by_z, 1 - half, 1, False)
        theirs = lax.ppermute(theirs, "seq", flip)

        inner, outer = last // 2, last - 2
        groups = [
            list(range(-inner, inner + 1)),
            list(range(-outer, -inner)) + list(range(inner + 1, outer + 1)),
            [1 - last, last - 1, last],
        ]

        def times(toks, weight, group):
            tok = jnp.concatenate([toks[(o + last) % n_z] for o in group], axis=0)
            return lax.dot_general(tok, weight, (((0,), (0,)), ((), ())), preferred_element_type=f32)

        def join(partial, keep):
            sent = lax.ppermute(partial.astype(jnp.bfloat16), "seq", flip)
            return keep + sent.astype(f32)

        columns = 3 * width
        sums = ()
        for group in groups[:2]:
            places = [(o + last) % n_z for o in group]
            sums = project(mine, theirs, sums, [pieces[o] for o in group], places, width)
        mine_sum, theirs_sum = sums
        final = jnp.concatenate([pieces[o] for o in groups[2]], axis=0)
        kv_cols, q_cols = slice(0, 2 * width), slice(2 * width, columns)
        away = theirs_sum[:, kv_cols] + times(theirs, final[:, kv_cols], groups[2])
        kv_proj = join(away, mine_sum[:, kv_cols] + times(mine, final[:, kv_cols], groups[2]))
        away = theirs_sum[:, q_cols] + times(theirs, final[:, q_cols], groups[2])
        q_proj = join(away, mine_sum[:, q_cols] + times(mine, final[:, q_cols], groups[2]))

        swaps = []
        batches = (groups[0], groups[1] + groups[2])
        for batch in batches:
            joined = jnp.concatenate([pieces[o][:, 3 * width :] for o in batch], axis=0)
            swaps.append(lax.ppermute(joined, "seq", flip))

        key = jax.nn.silu(kv_proj[:, :width]).astype(jnp.bfloat16).reshape(rows, heads, hsize)
        value = kv_proj[:, width:].astype(jnp.bfloat16).reshape(rows, heads, hsize)
        query = jax.nn.silu(q_proj).astype(jnp.bfloat16).reshape(rows, heads, hsize)
        cum = jnp.cumsum(log_decay, axis=1)
        scaled_key = (key.astype(f32) * jnp.exp(cum[:, -1:] - cum).T[:, :, None]).astype(jnp.bfloat16)
        local = jnp.einsum("thd,the->hde", scaled_key, value, preferred_element_type=f32)
        where = jnp.stack([z, half, core]).astype(jnp.int32)
        earlier_state, where = exclusive_state(local, cum[:, -1], n_seq, where)
        own_at = list(pieces)
        own = [pieces[o] for o in own_at]
        outs = place_outs(where, own, own_at, swaps, batches, n_z, shard, width)
        out_mine, out_theirs = outs[0], outs[1]

        later = jnp.arange(rows)[:, None] >= jnp.arange(rows)[None, :]
        scores = jnp.einsum("thd,shd->hts", query, key, preferred_element_type=f32)
        spread = cum[:, :, None] - cum[:, None, :]
        factor = jnp.where(later[None], jnp.exp(jnp.minimum(spread, 0.0)), 0.0)
        weights = (scores * factor).astype(jnp.bfloat16)
        intra = jnp.einsum("hts,shd->thd", weights, value, preferred_element_type=f32)
        intra = lax.optimization_barrier(intra)
        carried = jnp.einsum("thd,hde->the", query, earlier_state, preferred_element_type=f32)
        attn = intra + carried * jnp.exp(cum).T[:, :, None]
        power = jnp.mean(attn * attn, axis=-1, keepdims=True)
        gain = norm_gain.reshape(heads, hsize)
        normed = (attn / jnp.sqrt(power + 1e-05) * gain[None]).astype(jnp.bfloat16).reshape(rows, width)

        wide = jnp.broadcast_to(normed[None], (n_dp // 2, rows, width))
        give = jnp.einsum("itg,idg->itd", wide, out_theirs, preferred_element_type=f32)
        taken = lax.ppermute(give.astype(jnp.bfloat16), "dp", pair_perm(n_dp))
        keep = jnp.einsum("itg,idg->itd", wide, out_mine, preferred_element_type=f32)
        keep = lax.optimization_barrier(keep.astype(jnp.bfloat16)).astype(f32) + taken.astype(f32)
        groups = [[2 * i + c for i in range(n_dp // 2)] for c in range(2)]
        spread_out = lax.all_to_all(keep.astype(jnp.bfloat16), "dp", 0, 0, axis_index_groups=groups, tiled=True)
        return jnp.sum(spread_out.astype(f32), axis=0).astype(jnp.bfloat16)

    return layer


def solution(mesh):
    body = make_body(mesh.shape["seq"], mesh.shape["dp"])
    in_specs = (P("seq", None), P("seq", None, "dp"), P("seq", "dp"), P("dp", "seq"), P("dp"))
    return jax.shard_map(body, mesh=mesh, in_specs=in_specs, out_specs=P("seq", "dp"), check_vma=False)
```

```python
import jax
import jax.numpy as jnp
from jax import lax
from jax.sharding import PartitionSpec as P
from jax.experimental import pallas as pl
from jax.experimental.pallas import tpu as pltpu


def ring_perm(n, step):
    return [(s, (s + step) % n) for s in range(n)]


def pair_perm(n):
    return [(s, s ^ 1) for s in range(n)]


def exclusive_state(local, log_fall, n, where):
    heads, hsize, _ = local.shape
    rows = heads * hsize * hsize // (n * 128)
    pieces = local.astype(jnp.bfloat16).reshape(n, rows, 128)
    high = lax.reduce_precision(log_fall, 8, 7)
    middle = lax.reduce_precision(log_fall - high, 8, 7)
    low = lax.reduce_precision(log_fall - high - middle, 8, 7)
    falls = jnp.stack([high, middle, low], axis=1)
    falls = jnp.repeat(falls, n // heads, axis=0).astype(jnp.bfloat16)
    falls = jnp.pad(falls[:, None, :], ((0, 0), (0, rows - 1), (0, 128 - 3)))
    sent = jnp.concatenate([pieces, falls], axis=1)
    got = lax.all_to_all(sent, "seq", 0, 0, tiled=True)
    fall_of = jnp.sum(got[:, rows, :3].astype(jnp.float32), axis=1)
    at = jnp.arange(n)
    between = (at[None, None, :] > at[None, :, None]) & (at[None, None, :] < at[:, None, None])
    total = jnp.sum(jnp.where(between, fall_of[None, None, :], 0.0), axis=2)
    mix = jnp.where(at[None, :] < at[:, None], jnp.exp(total), 0.0)
    slices = got[:, :rows, :].reshape(n, rows * 128).astype(jnp.float32)
    earlier = jnp.dot(mix, slices, precision=lax.Precision.HIGHEST)
    earlier = earlier.astype(jnp.bfloat16).reshape(n, rows, 128)
    earlier, where = lax.optimization_barrier((earlier, where))
    back = lax.all_to_all(earlier, "seq", 0, 0, tiled=True)
    return back.reshape(heads, hsize, hsize), where


def whole(shape):
    return pl.BlockSpec(shape, lambda i: (0,) * len(shape), pipeline_mode=pl.Buffered(1))


def place_outs(where, own, swapped, batches, n_z, shard, width):
    def kernel(where_ref, *refs):
        out = refs[-1]
        z, half, core = where_ref[0], where_ref[1], where_ref[2]

        def place(block, offset, side):
            at = lax.rem(z + (offset + n_z), n_z)
            away = lax.rem(lax.rem(at, 2) + core, 2)
            rows = pl.ds(pl.multiple_of(side * shard, shard), shard)
            out[away, lax.div(at, 2), rows, :] = block

        for i, offsets in enumerate(batches):
            for n, offset in enumerate(offsets):
                rows = slice(n * shard, (n + 1) * shard)
                place(refs[i][rows, :], offset, half)
                place(refs[len(own) + i][rows, :], offset, 1 - half)

    shape = (2, n_z // 2, 2 * shard, width)
    return pl.pallas_call(
        kernel,
        out_shape=jax.ShapeDtypeStruct(shape, jnp.bfloat16),
        grid=(1,),
        in_specs=[pl.BlockSpec(memory_space=pltpu.SMEM)]
        + [whole(a.shape) for a in (*own, *swapped)],
        out_specs=whole(shape),
        compiler_params=pltpu.CompilerParams(vmem_limit_bytes=24 << 20),
        name="place_outs",
    )(where, *own, *swapped)


def pack_outs(pieces, width):
    def kernel(*refs):
        for n, ref in enumerate(refs[:-1]):
            refs[-1][n * shard : (n + 1) * shard, :] = ref[...]

    shard = pieces[0].shape[0]
    shape = (len(pieces) * shard, width)
    return pl.pallas_call(
        kernel,
        out_shape=jax.ShapeDtypeStruct(shape, jnp.bfloat16),
        grid=(1,),
        in_specs=[pl.BlockSpec((shard, width), lambda i: (0, 3), pipeline_mode=pl.Buffered(1))] * len(pieces),
        out_specs=whole(shape),
        compiler_params=pltpu.CompilerParams(vmem_limit_bytes=12 << 20),
        name="pack_outs",
    )(*pieces)


def project(mine, theirs, sums, pieces, places, width):
    def kernel(mine_ref, theirs_ref, *refs):
        weights, outs = refs[len(sums) : len(sums) + len(pieces)], refs[-2:]
        for n, (tok, out) in enumerate(zip((mine_ref, theirs_ref), outs)):
            total = refs[n][...] if sums else None
            for weight, place in zip(weights, places):
                part = lax.dot_general(
                    tok[place], weight[...], (((0,), (0,)), ((), ())), preferred_element_type=jnp.float32
                )
                total = part if total is None else total + part
            out[...] = total

    shard = pieces[0].shape[0]
    shape = (mine.shape[2], 3 * width)
    return pl.pallas_call(
        kernel,
        out_shape=[jax.ShapeDtypeStruct(shape, jnp.float32)] * 2,
        grid=(1,),
        in_specs=[whole(mine.shape)] * 2
        + [whole(shape)] * len(sums)
        + [pl.BlockSpec((shard, 3 * width), lambda i: (0, 0), pipeline_mode=pl.Buffered(1))] * len(pieces),
        out_specs=[whole(shape)] * 2,
        compiler_params=pltpu.CompilerParams(vmem_limit_bytes=32 << 20),
        name="project",
    )(mine, theirs, *sums, *pieces)


def make_body(n_seq, n_dp):
    n_z = n_seq // 2
    up, down, flip = ring_perm(n_seq, 2), ring_perm(n_seq, -2), pair_perm(n_seq)

    def layer(tokens, qkv_weight, out_weight, log_decay, norm_gain):
        rows, _ = tokens.shape
        width = qkv_weight.shape[2]
        heads = log_decay.shape[0]
        hsize = width // heads
        shard = qkv_weight.shape[0]
        place = lax.axis_index("seq")
        z, half = place // 2, place % 2
        core = lax.axis_index("dp") % 2
        f32 = jnp.float32

        parts = jnp.transpose(qkv_weight, (1, 0, 2))
        own = jnp.concatenate([parts[1], parts[2], parts[0], out_weight], axis=1)
        pieces = {0: own}
        last = n_z // 2
        ahead = behind = own
        for k in range(1, last):
            ahead = lax.ppermute(ahead, "seq", up)
            behind = lax.ppermute(behind, "seq", down)
            pieces[-k], pieces[k] = ahead, behind
        top = lax.ppermute(ahead[: shard // 2], "seq", up)
        bottom = lax.ppermute(behind[shard // 2 :], "seq", down)
        pieces[last] = jnp.concatenate([top, bottom], axis=0)

        by_z = tokens.T.reshape(n_z, 2, shard, rows)
        by_z, _ = lax.optimization_barrier((by_z, pieces[-1]))
        by_z = jnp.concatenate([by_z, by_z], axis=0)
        by_z = lax.dynamic_slice_in_dim(by_z, (z + last) % n_z, n_z, axis=0)
        mine = lax.dynamic_index_in_dim(by_z, half, 1, False)
        theirs = lax.dynamic_index_in_dim(by_z, 1 - half, 1, False)
        theirs = lax.ppermute(theirs, "seq", flip)

        inner, outer = last // 2, last - 2
        groups = [
            list(range(-inner, inner + 1)),
            list(range(-outer, -inner)) + list(range(inner + 1, outer + 1)),
            [1 - last, last - 1, last],
        ]

        def times(toks, weight, group):
            tok = jnp.concatenate([toks[(o + last) % n_z] for o in group], axis=0)
            return lax.dot_general(tok, weight, (((0,), (0,)), ((), ())), preferred_element_type=f32)

        def join(partial, keep):
            sent = lax.ppermute(partial.astype(jnp.bfloat16), "seq", flip)
            return keep + sent.astype(f32)

        columns = 3 * width
        known = groups[0] + groups[1]
        places = [(o + last) % n_z for o in known]
        sums = project(mine, theirs, (), [pieces[o] for o in known], places, width)
        mine_sum, theirs_sum = sums
        final = jnp.concatenate([pieces[o] for o in groups[2]], axis=0)
        kv_cols, q_cols = slice(0, 2 * width), slice(2 * width, columns)
        away = theirs_sum[:, kv_cols] + times(theirs, final[:, kv_cols], groups[2])
        kv_proj = join(away, mine_sum[:, kv_cols] + times(mine, final[:, kv_cols], groups[2]))
        away = theirs_sum[:, q_cols] + times(theirs, final[:, q_cols], groups[2])
        q_proj = join(away, mine_sum[:, q_cols] + times(mine, final[:, q_cols], groups[2]))

        swaps, packs = [], []
        first, second = last // 2 - 1, last // 2 + 1
        batches = (
            list(range(-first, first + 1)),
            list(range(-second, -first)) + list(range(first + 1, second + 1)),
            list(range(1 - last, -second)) + list(range(second + 1, last + 1)),
        )
        for n, batch in enumerate(batches):
            packs.append(pack_outs([pieces[o] for o in batch], width))
            swaps.append(lax.ppermute(packs[n], "seq", flip))

        key = jax.nn.silu(kv_proj[:, :width]).astype(jnp.bfloat16).reshape(rows, heads, hsize)
        value = kv_proj[:, width:].astype(jnp.bfloat16).reshape(rows, heads, hsize)
        query = jax.nn.silu(q_proj).astype(jnp.bfloat16).reshape(rows, heads, hsize)
        cum = jnp.cumsum(log_decay, axis=1)
        scaled_key = (key.astype(f32) * jnp.exp(cum[:, -1:] - cum).T[:, :, None]).astype(jnp.bfloat16)
        local = jnp.einsum("thd,the->hde", scaled_key, value, preferred_element_type=f32)
        where = jnp.stack([z, half, core]).astype(jnp.int32)
        earlier_state, where = exclusive_state(local, cum[:, -1], n_seq, where)
        outs = place_outs(where, packs, swaps, batches, n_z, shard, width)
        out_mine, out_theirs = outs[0], outs[1]

        later = jnp.arange(rows)[:, None] >= jnp.arange(rows)[None, :]
        scores = jnp.einsum("thd,shd->hts", query, key, preferred_element_type=f32)
        spread = cum[:, :, None] - cum[:, None, :]
        factor = jnp.where(later[None], jnp.exp(jnp.minimum(spread, 0.0)), 0.0)
        weights = (scores * factor).astype(jnp.bfloat16)
        intra = jnp.einsum("hts,shd->thd", weights, value, preferred_element_type=f32)
        intra = lax.optimization_barrier(intra)
        carried = jnp.einsum("thd,hde->the", query, earlier_state, preferred_element_type=f32)
        attn = intra + carried * jnp.exp(cum).T[:, :, None]
        power = jnp.mean(attn * attn, axis=-1, keepdims=True)
        gain = norm_gain.reshape(heads, hsize)
        normed = (attn / jnp.sqrt(power + 1e-05) * gain[None]).astype(jnp.bfloat16).reshape(rows, width)

        wide = jnp.broadcast_to(normed[None], (n_dp // 2, rows, width))
        give = jnp.einsum("itg,idg->itd", wide, out_theirs, preferred_element_type=f32)
        taken = lax.ppermute(give.astype(jnp.bfloat16), "dp", pair_perm(n_dp))
        keep = jnp.einsum("itg,idg->itd", wide, out_mine, preferred_element_type=f32)
        keep = lax.optimization_barrier(keep.astype(jnp.bfloat16)).astype(f32) + taken.astype(f32)
        groups = [[2 * i + c for i in range(n_dp // 2)] for c in range(2)]
        spread_out = lax.all_to_all(keep.astype(jnp.bfloat16), "dp", 0, 0, axis_index_groups=groups, tiled=True)
        return jnp.sum(spread_out.astype(f32), axis=0).astype(jnp.bfloat16)

    return layer


def solution(mesh):
    body = make_body(mesh.shape["seq"], mesh.shape["dp"])
    in_specs = (P("seq", None), P("seq", None, "dp"), P("seq", "dp"), P("dp", "seq"), P("dp"))
    return jax.shard_map(body, mesh=mesh, in_specs=in_specs, out_specs=P("seq", "dp"), check_vma=False)
```

```python
import jax
import jax.numpy as jnp
from jax import lax
from jax.sharding import PartitionSpec as P
from jax.experimental import pallas as pl
from jax.experimental.pallas import tpu as pltpu


def ring_perm(n, step):
    return [(s, (s + step) % n) for s in range(n)]


def pair_perm(n):
    return [(s, s ^ 1) for s in range(n)]


def exclusive_state(local, log_fall, n, where):
    heads, hsize, _ = local.shape
    rows = heads * hsize * hsize // (n * 128)
    pieces = local.astype(jnp.bfloat16).reshape(n, rows, 128)
    high = lax.reduce_precision(log_fall, 8, 7)
    middle = lax.reduce_precision(log_fall - high, 8, 7)
    low = lax.reduce_precision(log_fall - high - middle, 8, 7)
    falls = jnp.stack([high, middle, low], axis=1)
    falls = jnp.repeat(falls, n // heads, axis=0).astype(jnp.bfloat16)
    falls = jnp.pad(falls[:, None, :], ((0, 0), (0, rows - 1), (0, 128 - 3)))
    sent = jnp.concatenate([pieces, falls], axis=1)
    got = lax.all_to_all(sent, "seq", 0, 0, tiled=True)
    fall_of = jnp.sum(got[:, rows, :3].astype(jnp.float32), axis=1)
    at = jnp.arange(n)
    between = (at[None, None, :] > at[None, :, None]) & (at[None, None, :] < at[:, None, None])
    total = jnp.sum(jnp.where(between, fall_of[None, None, :], 0.0), axis=2)
    mix = jnp.where(at[None, :] < at[:, None], jnp.exp(total), 0.0)
    slices = got[:, :rows, :].reshape(n, rows * 128).astype(jnp.float32)
    earlier = jnp.dot(mix, slices, precision=lax.Precision.HIGHEST)
    earlier = earlier.astype(jnp.bfloat16).reshape(n, rows, 128)
    earlier, where = lax.optimization_barrier((earlier, where))
    back = lax.all_to_all(earlier, "seq", 0, 0, tiled=True)
    return back.reshape(heads, hsize, hsize), where


def in_hbm(x):
    return pltpu.with_memory_space_constraint(x, pltpu.HBM)


def whole(shape):
    return pl.BlockSpec(shape, lambda i: (0,) * len(shape), pipeline_mode=pl.Buffered(1))


def place_outs(where, own, swapped, batches, n_z, shard, width):
    def kernel(where_ref, *refs):
        out = refs[-1]
        z, half, core = where_ref[0], where_ref[1], where_ref[2]

        def place(block, offset, side):
            at = lax.rem(z + (offset + n_z), n_z)
            away = lax.rem(lax.rem(at, 2) + core, 2)
            rows = pl.ds(pl.multiple_of(side * shard, shard), shard)
            out[away, lax.div(at, 2), rows, :] = block

        for i, offsets in enumerate(batches):
            for n, offset in enumerate(offsets):
                rows = slice(n * shard, (n + 1) * shard)
                place(refs[i][rows, :], offset, half)
                place(refs[len(own) + i][rows, :], offset, 1 - half)

    shape = (2, n_z // 2, 2 * shard, width)
    return pl.pallas_call(
        kernel,
        out_shape=jax.ShapeDtypeStruct(shape, jnp.bfloat16),
        grid=(1,),
        in_specs=[pl.BlockSpec(memory_space=pltpu.SMEM)]
        + [whole(a.shape) for a in (*own, *swapped)],
        out_specs=whole(shape),
        compiler_params=pltpu.CompilerParams(vmem_limit_bytes=12 << 20),
        name="place_outs",
    )(where, *own, *swapped)


def pack_outs(pieces, width):
    def kernel(*refs):
        for n, ref in enumerate(refs[:-1]):
            refs[-1][n * shard : (n + 1) * shard, :] = ref[...]

    shard = pieces[0].shape[0]
    shape = (len(pieces) * shard, width)
    return pl.pallas_call(
        kernel,
        out_shape=jax.ShapeDtypeStruct(shape, jnp.bfloat16),
        grid=(1,),
        in_specs=[pl.BlockSpec((shard, width), lambda i: (0, 3), pipeline_mode=pl.Buffered(1))] * len(pieces),
        out_specs=whole(shape),
        compiler_params=pltpu.CompilerParams(vmem_limit_bytes=6 << 20),
        name="pack_outs",
    )(*[in_hbm(p) for p in pieces])


def project(where, toks, sums, blocks, jobs, n_z, columns):
    def kernel(where_ref, *refs):
        tok_refs, refs = refs[: len(toks)], refs[len(toks) :]
        sum_refs, refs = refs[: len(sums)], refs[len(sums) :]
        for (tok, base, lo, hi, kind), out in zip(jobs, refs[len(blocks) :]):
            total = None if base is None else sum_refs[base][:, lo:hi]
            for (_, offset, row, count), weight in zip(blocks, refs):
                at = lax.rem(where_ref[0] + (offset + n_z), n_z)
                part = lax.dot_general(
                    tok_refs[tok][at, row : row + count, :],
                    weight[:, lo:hi],
                    (((0,), (0,)), ((), ())),
                    preferred_element_type=jnp.float32,
                )
                total = part if total is None else total + part
            out[...] = total.astype(kind)

    rows = toks[0].shape[2]
    return pl.pallas_call(
        kernel,
        out_shape=[jax.ShapeDtypeStruct((rows, hi - lo), kind) for _, _, lo, hi, kind in jobs],
        grid=(1,),
        in_specs=[pl.BlockSpec(memory_space=pltpu.SMEM)]
        + [whole(a.shape) for a in (*toks, *sums)]
        + [
            pl.BlockSpec((count, columns), lambda i: (0, 0), pipeline_mode=pl.Buffered(1))
            for _, _, _, count in blocks
        ],
        out_specs=[whole((rows, hi - lo)) for _, _, lo, hi, _ in jobs],
        compiler_params=pltpu.CompilerParams(vmem_limit_bytes=16 << 20),
        name="project",
    )(where, *toks, *sums, *[block[0] if sums else in_hbm(block[0]) for block in blocks])


def make_body(n_seq, n_dp):
    n_z = n_seq // 2
    up, down, flip = ring_perm(n_seq, 2), ring_perm(n_seq, -2), pair_perm(n_seq)

    def layer(tokens, qkv_weight, out_weight, log_decay, norm_gain):
        rows, _ = tokens.shape
        width = qkv_weight.shape[2]
        heads = log_decay.shape[0]
        hsize = width // heads
        shard = qkv_weight.shape[0]
        place = lax.axis_index("seq")
        z, half = place // 2, place % 2
        core = lax.axis_index("dp") % 2
        f32 = jnp.float32

        parts = jnp.transpose(qkv_weight, (1, 0, 2))
        own = jnp.concatenate([parts[1], parts[2], parts[0], out_weight], axis=1)
        pieces = {0: own}
        last = n_z // 2
        ahead = behind = own
        for k in range(1, last):
            ahead = lax.ppermute(ahead, "seq", up)
            behind = lax.ppermute(behind, "seq", down)
            pieces[-k], pieces[k] = ahead, behind
        top = lax.ppermute(ahead[: shard // 2], "seq", up)
        bottom = lax.ppermute(behind[shard // 2 :], "seq", down)
        pieces[last] = jnp.concatenate([top, bottom], axis=0)

        by_z = tokens.T.reshape(n_z, 2, shard, rows)
        by_z, _ = lax.optimization_barrier((by_z, pieces[-1]))
        mine = lax.dynamic_index_in_dim(by_z, half, 1, False)
        theirs = lax.dynamic_index_in_dim(by_z, 1 - half, 1, False)
        theirs = lax.ppermute(theirs, "seq", flip)

        inner, outer = last // 2, last - 2
        groups = [
            list(range(-inner, inner + 1)),
            list(range(-outer, -inner)) + list(range(inner + 1, outer + 1)),
            [1 - last, last - 1, last],
        ]

        columns = 3 * width
        where = jnp.stack([z, half, core]).astype(jnp.int32)
        toks = (mine, theirs)
        known = [(pieces[o], o, 0, shard) for o in groups[0] + groups[1]]
        final = [(pieces[o], o, 0, shard) for o in groups[2][:2]]
        final += [(top, last, 0, shard // 2), (bottom, last, shard // 2, shard // 2)]
        b16, kv = jnp.bfloat16, 2 * width
        jobs = [(0, None, 0, columns, f32), (1, None, 0, columns, f32)]
        sums = project(where, toks, (), known, jobs, n_z, columns)
        (away,) = project(where, (theirs,), sums[1:], final, [(0, 0, 0, kv, b16)], n_z, columns)
        sent = lax.ppermute(away, "seq", flip)
        jobs = [(0, 0, 0, kv, f32), (0, 0, kv, columns, f32), (1, 1, kv, columns, b16)]
        kept_kv, kept_q, away = project(where, toks, sums, final, jobs, n_z, columns)
        kv_proj = kept_kv + sent.astype(f32)
        q_proj = kept_q + lax.ppermute(away, "seq", flip).astype(f32)

        swaps, packs = [], []
        first, second = last // 2 - 1, last // 2 + 1
        batches = (
            list(range(-first, first + 1)),
            list(range(-second, -first)) + list(range(first + 1, second + 1)),
            list(range(1 - last, -second)) + list(range(second + 1, last + 1)),
        )
        for n, batch in enumerate(batches):
            packs.append(pack_outs([pieces[o] for o in batch], width))
            swaps.append(lax.ppermute(packs[n], "seq", flip))

        key = jax.nn.silu(kv_proj[:, :width]).astype(jnp.bfloat16).reshape(rows, heads, hsize)
        value = kv_proj[:, width:].astype(jnp.bfloat16).reshape(rows, heads, hsize)
        query = jax.nn.silu(q_proj).astype(jnp.bfloat16).reshape(rows, heads, hsize)
        cum = jnp.cumsum(log_decay, axis=1)
        scaled_key = (key.astype(f32) * jnp.exp(cum[:, -1:] - cum).T[:, :, None]).astype(jnp.bfloat16)
        local = jnp.einsum("thd,the->hde", scaled_key, value, preferred_element_type=f32)
        earlier_state, where = exclusive_state(local, cum[:, -1], n_seq, where)
        outs = place_outs(where, packs, swaps, batches, n_z, shard, width)
        out_mine, out_theirs = outs[0], outs[1]

        later = jnp.arange(rows)[:, None] >= jnp.arange(rows)[None, :]
        scores = jnp.einsum("thd,shd->hts", query, key, preferred_element_type=f32)
        spread = cum[:, :, None] - cum[:, None, :]
        factor = jnp.where(later[None], jnp.exp(jnp.minimum(spread, 0.0)), 0.0)
        weights = (scores * factor).astype(jnp.bfloat16)
        intra = jnp.einsum("hts,shd->thd", weights, value, preferred_element_type=f32)
        intra = lax.optimization_barrier(intra)
        carried = jnp.einsum("thd,hde->the", query, earlier_state, preferred_element_type=f32)
        attn = intra + carried * jnp.exp(cum).T[:, :, None]
        power = jnp.mean(attn * attn, axis=-1, keepdims=True)
        gain = norm_gain.reshape(heads, hsize)
        normed = (attn / jnp.sqrt(power + 1e-05) * gain[None]).astype(jnp.bfloat16).reshape(rows, width)

        wide = jnp.broadcast_to(normed[None], (n_dp // 2, rows, width))
        give = jnp.einsum("itg,idg->itd", wide, out_theirs, preferred_element_type=f32)
        taken = lax.ppermute(give.astype(jnp.bfloat16), "dp", pair_perm(n_dp))
        keep = jnp.einsum("itg,idg->itd", wide, out_mine, preferred_element_type=f32)
        keep = lax.optimization_barrier(keep.astype(jnp.bfloat16)).astype(f32) + taken.astype(f32)
        groups = [[2 * i + c for i in range(n_dp // 2)] for c in range(2)]
        spread_out = lax.all_to_all(keep.astype(jnp.bfloat16), "dp", 0, 0, axis_index_groups=groups, tiled=True)
        return jnp.sum(spread_out.astype(f32), axis=0).astype(jnp.bfloat16)

    return layer


def solution(mesh):
    body = make_body(mesh.shape["seq"], mesh.shape["dp"])
    in_specs = (P("seq", None), P("seq", None, "dp"), P("seq", "dp"), P("dp", "seq"), P("dp"))
    return jax.shard_map(body, mesh=mesh, in_specs=in_specs, out_specs=P("seq", "dp"), check_vma=False)
```

```python
import jax
import jax.numpy as jnp
from jax import lax
from jax.sharding import PartitionSpec as P
from jax.experimental import pallas as pl
from jax.experimental.pallas import tpu as pltpu


def ring_perm(n, step):
    return [(s, (s + step) % n) for s in range(n)]


def pair_perm(n):
    return [(s, s ^ 1) for s in range(n)]


def exclusive_state(local, log_fall, n, where):
    heads, hsize, _ = local.shape
    rows = heads * hsize * hsize // (n * 128)
    pieces = local.astype(jnp.bfloat16).reshape(n, rows, 128)
    high = lax.reduce_precision(log_fall, 8, 7)
    middle = lax.reduce_precision(log_fall - high, 8, 7)
    low = lax.reduce_precision(log_fall - high - middle, 8, 7)
    falls = jnp.stack([high, middle, low], axis=1)
    falls = jnp.repeat(falls, n // heads, axis=0).astype(jnp.bfloat16)
    falls = jnp.pad(falls[:, None, :], ((0, 0), (0, rows - 1), (0, 128 - 3)))
    sent = jnp.concatenate([pieces, falls], axis=1)
    got = lax.all_to_all(sent, "seq", 0, 0, tiled=True)
    fall_of = jnp.sum(got[:, rows, :3].astype(jnp.float32), axis=1)
    at = jnp.arange(n)
    between = (at[None, None, :] > at[None, :, None]) & (at[None, None, :] < at[:, None, None])
    total = jnp.sum(jnp.where(between, fall_of[None, None, :], 0.0), axis=2)
    mix = jnp.where(at[None, :] < at[:, None], jnp.exp(total), 0.0)
    slices = got[:, :rows, :].reshape(n, rows * 128).astype(jnp.float32)
    earlier = jnp.dot(mix, slices, precision=lax.Precision.HIGHEST)
    earlier = earlier.astype(jnp.bfloat16).reshape(n, rows, 128)
    earlier, where = lax.optimization_barrier((earlier, where))
    back = lax.all_to_all(earlier, "seq", 0, 0, tiled=True)
    return back.reshape(heads, hsize, hsize), where


def in_hbm(x):
    return pltpu.with_memory_space_constraint(x, pltpu.HBM)


def whole(shape):
    return pl.BlockSpec(shape, lambda i: (0,) * len(shape), pipeline_mode=pl.Buffered(1))


def place_outs(where, own, swapped, batches, n_z, shard, width):
    def kernel(where_ref, *refs):
        out = refs[-1]
        z, half, core = where_ref[0], where_ref[1], where_ref[2]

        def place(block, offset, side):
            at = lax.rem(z + (offset + n_z), n_z)
            away = lax.rem(lax.rem(at, 2) + core, 2)
            rows = pl.ds(pl.multiple_of(side * shard, shard), shard)
            out[away, lax.div(at, 2), rows, :] = block

        for i, offsets in enumerate(batches):
            for n, offset in enumerate(offsets):
                rows = slice(n * shard, (n + 1) * shard)
                place(refs[i][rows, :], offset, half)
                place(refs[len(own) + i][rows, :], offset, 1 - half)

    shape = (2, n_z // 2, 2 * shard, width)
    return pl.pallas_call(
        kernel,
        out_shape=jax.ShapeDtypeStruct(shape, jnp.bfloat16),
        grid=(1,),
        in_specs=[pl.BlockSpec(memory_space=pltpu.SMEM)]
        + [whole(a.shape) for a in (*own, *swapped)],
        out_specs=whole(shape),
        compiler_params=pltpu.CompilerParams(vmem_limit_bytes=12 << 20),
        name="place_outs",
    )(where, *own, *swapped)


def pack_outs(pieces, width):
    def kernel(*refs):
        for n, ref in enumerate(refs[:-1]):
            refs[-1][n * shard : (n + 1) * shard, :] = ref[...]

    shard = pieces[0].shape[0]
    shape = (len(pieces) * shard, width)
    return pl.pallas_call(
        kernel,
        out_shape=jax.ShapeDtypeStruct(shape, jnp.bfloat16),
        grid=(1,),
        in_specs=[pl.BlockSpec((shard, width), lambda i: (0, 3), pipeline_mode=pl.Buffered(1))] * len(pieces),
        out_specs=whole(shape),
        compiler_params=pltpu.CompilerParams(vmem_limit_bytes=6 << 20),
        name="pack_outs",
    )(*[in_hbm(p) for p in pieces])


def project(where, toks, sums, blocks, jobs, n_z, columns):
    def kernel(where_ref, *refs):
        tok_refs, refs = refs[: len(toks)], refs[len(toks) :]
        sum_refs, refs = refs[: len(sums)], refs[len(sums) :]
        for (tok, base, lo, hi, kind), out in zip(jobs, refs[len(blocks) :]):
            total = None if base is None else sum_refs[base][:, lo:hi]
            for (_, offset, row, count), weight in zip(blocks, refs):
                at = lax.rem(where_ref[0] + (offset + n_z), n_z)
                part = lax.dot_general(
                    tok_refs[tok][at, row : row + count, :],
                    weight[:, lo:hi],
                    (((0,), (0,)), ((), ())),
                    preferred_element_type=jnp.float32,
                )
                total = part if total is None else total + part
            out[...] = total.astype(kind)

    rows = toks[0].shape[2]
    return pl.pallas_call(
        kernel,
        out_shape=[jax.ShapeDtypeStruct((rows, hi - lo), kind) for _, _, lo, hi, kind in jobs],
        grid=(1,),
        in_specs=[pl.BlockSpec(memory_space=pltpu.SMEM)]
        + [whole(a.shape) for a in (*toks, *sums)]
        + [
            pl.BlockSpec((count, columns), lambda i: (0, 0), pipeline_mode=pl.Buffered(1))
            for _, _, _, count in blocks
        ],
        out_specs=[whole((rows, hi - lo)) for _, _, lo, hi, _ in jobs],
        compiler_params=pltpu.CompilerParams(vmem_limit_bytes=16 << 20),
        name="project",
    )(where, *toks, *sums, *[block[0] if sums else in_hbm(block[0]) for block in blocks])


def make_body(n_seq, n_dp):
    n_z = n_seq // 2
    up, down, flip = ring_perm(n_seq, 2), ring_perm(n_seq, -2), pair_perm(n_seq)

    def layer(tokens, qkv_weight, out_weight, log_decay, norm_gain):
        rows, _ = tokens.shape
        width = qkv_weight.shape[2]
        heads = log_decay.shape[0]
        hsize = width // heads
        shard = qkv_weight.shape[0]
        place = lax.axis_index("seq")
        z, half = place // 2, place % 2
        core = lax.axis_index("dp") % 2
        f32 = jnp.float32

        parts = jnp.transpose(qkv_weight, (1, 0, 2))
        own = jnp.concatenate([parts[1], parts[2], parts[0], out_weight], axis=1)
        by_z = tokens.T.reshape(n_z, 2, shard, rows)
        mine = lax.dynamic_index_in_dim(by_z, half, 1, False)
        theirs = lax.dynamic_index_in_dim(by_z, 1 - half, 1, False)

        pieces = {0: own}
        last = n_z // 2
        ahead = behind = own
        for k in range(1, last):
            ahead = lax.ppermute(ahead, "seq", up)
            behind = lax.ppermute(behind, "seq", down)
            if k == 1:
                ahead, mine, theirs = lax.optimization_barrier((ahead, mine, theirs))
            pieces[-k], pieces[k] = ahead, behind
        top = lax.ppermute(ahead[: shard // 2], "seq", up)
        bottom = lax.ppermute(behind[shard // 2 :], "seq", down)
        pieces[last] = jnp.concatenate([top, bottom], axis=0)

        theirs = lax.ppermute(theirs, "seq", flip)

        inner, outer = last // 2, last - 2
        groups = [
            list(range(-inner, inner + 1)),
            list(range(-outer, -inner)) + list(range(inner + 1, outer + 1)),
            [1 - last, last - 1, last],
        ]

        columns = 3 * width
        where = jnp.stack([z, half, core]).astype(jnp.int32)
        toks = (mine, theirs)
        known = [(pieces[o], o, 0, shard) for o in groups[0] + groups[1]]
        kv = 2 * width
        jobs = [(0, None, 0, columns, f32), (1, None, 0, columns, f32)]
        mine_sum, theirs_sum = project(where, toks, (), known, jobs, n_z, columns)
        final = jnp.concatenate([pieces[groups[2][0]], pieces[groups[2][1]], top, bottom], axis=0)

        def add_final(total, tok, lo, hi):
            picked = [lax.dynamic_index_in_dim(tok, (z + o + n_z) % n_z, 0, False) for o in groups[2]]
            part = lax.dot_general(
                jnp.concatenate(picked, axis=0),
                final[:, lo:hi],
                (((0,), (0,)), ((), ())),
                preferred_element_type=f32,
            )
            return total[:, lo:hi] + part

        sent = lax.ppermute(add_final(theirs_sum, theirs, 0, kv).astype(jnp.bfloat16), "seq", flip)
        kv_proj = add_final(mine_sum, mine, 0, kv) + sent.astype(f32)
        q_away = add_final(theirs_sum, theirs, kv, columns).astype(jnp.bfloat16)

        swaps, packs = [], []
        first, second = last // 2 - 1, last // 2 + 1
        batches = (
            list(range(-first, first + 1)),
            list(range(-second, -first)) + list(range(first + 1, second + 1)),
            list(range(1 - last, -second)) + list(range(second + 1, last + 1)),
        )
        for n, batch in enumerate(batches):
            packs.append(pack_outs([pieces[o] for o in batch], width))
            if n < 2:
                swaps.append(lax.ppermute(packs[n], "seq", flip))
            else:
                joined = jnp.concatenate([packs[n], q_away], axis=0)
                swaps.append(lax.ppermute(joined, "seq", flip))
        q_proj = add_final(mine_sum, mine, kv, columns) + swaps[2][packs[2].shape[0] :].astype(f32)

        key = jax.nn.silu(kv_proj[:, :width]).astype(jnp.bfloat16).reshape(rows, heads, hsize)
        value = kv_proj[:, width:].astype(jnp.bfloat16).reshape(rows, heads, hsize)
        query = jax.nn.silu(q_proj).astype(jnp.bfloat16).reshape(rows, heads, hsize)
        cum = jnp.cumsum(log_decay, axis=1)
        scaled_key = (key.astype(f32) * jnp.exp(cum[:, -1:] - cum).T[:, :, None]).astype(jnp.bfloat16)
        local = jnp.einsum("thd,the->hde", scaled_key, value, preferred_element_type=f32)
        earlier_state, where = exclusive_state(local, cum[:, -1], n_seq, where)
        outs = place_outs(where, packs, swaps, batches, n_z, shard, width)
        out_mine, out_theirs = outs[0], outs[1]

        later = jnp.arange(rows)[:, None] >= jnp.arange(rows)[None, :]
        scores = jnp.einsum("thd,shd->hts", query, key, preferred_element_type=f32)
        spread = cum[:, :, None] - cum[:, None, :]
        factor = jnp.where(later[None], jnp.exp(jnp.minimum(spread, 0.0)), 0.0)
        weights = (scores * factor).astype(jnp.bfloat16)
        intra = jnp.einsum("hts,shd->thd", weights, value, preferred_element_type=f32)
        intra = lax.optimization_barrier(intra)
        carried = jnp.einsum("thd,hde->the", query, earlier_state, preferred_element_type=f32)
        attn = intra + carried * jnp.exp(cum).T[:, :, None]
        power = jnp.mean(attn * attn, axis=-1, keepdims=True)
        gain = norm_gain.reshape(heads, hsize)
        normed = (attn / jnp.sqrt(power + 1e-05) * gain[None]).astype(jnp.bfloat16).reshape(rows, width)

        wide = jnp.broadcast_to(normed[None], (n_dp // 2, rows, width))
        give = jnp.einsum("itg,idg->itd", wide, out_theirs, preferred_element_type=f32)
        taken = lax.ppermute(give.astype(jnp.bfloat16), "dp", pair_perm(n_dp))
        keep = jnp.einsum("itg,idg->itd", wide, out_mine, preferred_element_type=f32)
        keep = lax.optimization_barrier(keep.astype(jnp.bfloat16)).astype(f32) + taken.astype(f32)
        groups = [[2 * i + c for i in range(n_dp // 2)] for c in range(2)]
        spread_out = lax.all_to_all(keep.astype(jnp.bfloat16), "dp", 0, 0, axis_index_groups=groups, tiled=True)
        return jnp.sum(spread_out.astype(f32), axis=0).astype(jnp.bfloat16)

    return layer


def solution(mesh):
    body = make_body(mesh.shape["seq"], mesh.shape["dp"])
    in_specs = (P("seq", None), P("seq", None, "dp"), P("seq", "dp"), P("dp", "seq"), P("dp"))
    return jax.shard_map(body, mesh=mesh, in_specs=in_specs, out_specs=P("seq", "dp"), check_vma=False)
```

```python
import jax
import jax.numpy as jnp
from jax import lax
from jax.sharding import PartitionSpec as P
from jax.experimental import pallas as pl
from jax.experimental.pallas import tpu as pltpu


def ring_perm(n, step):
    return [(s, (s + step) % n) for s in range(n)]


def pair_perm(n):
    return [(s, s ^ 1) for s in range(n)]


def exclusive_state(local, log_fall, n, where):
    heads, hsize, _ = local.shape
    rows = heads * hsize * hsize // (n * 128)
    pieces = local.astype(jnp.bfloat16).reshape(n, rows, 128)
    high = lax.reduce_precision(log_fall, 8, 7)
    middle = lax.reduce_precision(log_fall - high, 8, 7)
    low = lax.reduce_precision(log_fall - high - middle, 8, 7)
    falls = jnp.stack([high, middle, low], axis=1)
    falls = jnp.repeat(falls, n // heads, axis=0).astype(jnp.bfloat16)
    falls = jnp.pad(falls[:, None, :], ((0, 0), (0, rows - 1), (0, 128 - 3)))
    sent = jnp.concatenate([pieces, falls], axis=1)
    got = lax.all_to_all(sent, "seq", 0, 0, tiled=True)
    fall_of = jnp.sum(got[:, rows, :3].astype(jnp.float32), axis=1)
    at = jnp.arange(n)
    between = (at[None, None, :] > at[None, :, None]) & (at[None, None, :] < at[:, None, None])
    total = jnp.sum(jnp.where(between, fall_of[None, None, :], 0.0), axis=2)
    mix = jnp.where(at[None, :] < at[:, None], jnp.exp(total), 0.0)
    slices = got[:, :rows, :].reshape(n, rows * 128).astype(jnp.float32)
    earlier = jnp.dot(mix, slices, precision=lax.Precision.HIGHEST)
    earlier = earlier.astype(jnp.bfloat16).reshape(n, rows, 128)
    earlier, where = lax.optimization_barrier((earlier, where))
    back = lax.all_to_all(earlier, "seq", 0, 0, tiled=True)
    return back.reshape(heads, hsize, hsize), where


def in_hbm(x):
    return pltpu.with_memory_space_constraint(x, pltpu.HBM)


def whole(shape):
    return pl.BlockSpec(shape, lambda i: (0,) * len(shape), pipeline_mode=pl.Buffered(1))


def place_outs(where, own, swapped, batches, n_z, shard, width):
    def kernel(where_ref, *refs):
        out = refs[-1]
        z, half, core = where_ref[0], where_ref[1], where_ref[2]

        def place(block, offset, side):
            at = lax.rem(z + (offset + n_z), n_z)
            away = lax.rem(lax.rem(at, 2) + core, 2)
            rows = pl.ds(pl.multiple_of(side * shard, shard), shard)
            out[away, lax.div(at, 2), rows, :] = block

        for i, offsets in enumerate(batches):
            for n, offset in enumerate(offsets):
                rows = slice(n * shard, (n + 1) * shard)
                place(refs[i][rows, :], offset, half)
                place(refs[len(own) + i][rows, :], offset, 1 - half)

    shape = (2, n_z // 2, 2 * shard, width)
    return pl.pallas_call(
        kernel,
        out_shape=jax.ShapeDtypeStruct(shape, jnp.bfloat16),
        grid=(1,),
        in_specs=[pl.BlockSpec(memory_space=pltpu.SMEM)]
        + [whole(a.shape) for a in (*own, *swapped)],
        out_specs=whole(shape),
        compiler_params=pltpu.CompilerParams(vmem_limit_bytes=12 << 20),
        name="place_outs",
    )(where, *own, *swapped)


def pack_outs(pieces, width):
    def kernel(*refs):
        for n, ref in enumerate(refs[:-1]):
            refs[-1][n * shard : (n + 1) * shard, :] = ref[...]

    shard = pieces[0].shape[0]
    shape = (len(pieces) * shard, width)
    return pl.pallas_call(
        kernel,
        out_shape=jax.ShapeDtypeStruct(shape, jnp.bfloat16),
        grid=(1,),
        in_specs=[pl.BlockSpec((shard, width), lambda i: (0, 3), pipeline_mode=pl.Buffered(1))] * len(pieces),
        out_specs=whole(shape),
        compiler_params=pltpu.CompilerParams(vmem_limit_bytes=6 << 20),
        name="pack_outs",
    )(*[in_hbm(p) for p in pieces])


def project(where, toks, sums, blocks, jobs, n_z, columns):
    def kernel(where_ref, *refs):
        tok_refs, refs = refs[: len(toks)], refs[len(toks) :]
        sum_refs, refs = refs[: len(sums)], refs[len(sums) :]
        for (tok, base, lo, hi, kind), out in zip(jobs, refs[len(blocks) :]):
            total = None if base is None else sum_refs[base][:, lo:hi]
            for (_, offset, row, count), weight in zip(blocks, refs):
                at = lax.rem(where_ref[0] + (offset + n_z), n_z)
                part = lax.dot_general(
                    tok_refs[tok][at, row : row + count, :],
                    weight[:, lo:hi],
                    (((0,), (0,)), ((), ())),
                    preferred_element_type=jnp.float32,
                )
                total = part if total is None else total + part
            out[...] = total.astype(kind)

    rows = toks[0].shape[2]
    return pl.pallas_call(
        kernel,
        out_shape=[jax.ShapeDtypeStruct((rows, hi - lo), kind) for _, _, lo, hi, kind in jobs],
        grid=(1,),
        in_specs=[pl.BlockSpec(memory_space=pltpu.SMEM)]
        + [whole(a.shape) for a in (*toks, *sums)]
        + [
            pl.BlockSpec((count, columns), lambda i: (0, 0), pipeline_mode=pl.Buffered(1))
            for _, _, _, count in blocks
        ],
        out_specs=[whole((rows, hi - lo)) for _, _, lo, hi, _ in jobs],
        compiler_params=pltpu.CompilerParams(vmem_limit_bytes=16 << 20),
        name="project",
    )(where, *toks, *sums, *[in_hbm(block[0]) for block in blocks])


def make_body(n_seq, n_dp):
    n_z = n_seq // 2
    up, down, flip = ring_perm(n_seq, 2), ring_perm(n_seq, -2), pair_perm(n_seq)

    def layer(tokens, qkv_weight, out_weight, log_decay, norm_gain):
        rows, _ = tokens.shape
        width = qkv_weight.shape[2]
        heads = log_decay.shape[0]
        hsize = width // heads
        shard = qkv_weight.shape[0]
        place = lax.axis_index("seq")
        z, half = place // 2, place % 2
        core = lax.axis_index("dp") % 2
        f32 = jnp.float32

        parts = jnp.transpose(qkv_weight, (1, 0, 2))
        own = jnp.concatenate([parts[1], parts[2], parts[0], out_weight], axis=1)
        by_z = tokens.T.reshape(n_z, 2, shard, rows)
        mine = lax.dynamic_index_in_dim(by_z, half, 1, False)
        theirs = lax.dynamic_index_in_dim(by_z, 1 - half, 1, False)

        pieces = {0: own}
        last = n_z // 2
        ahead = behind = own
        for k in range(1, last):
            ahead = lax.ppermute(ahead, "seq", up)
            behind = lax.ppermute(behind, "seq", down)
            if k == 1:
                ahead, mine, theirs = lax.optimization_barrier((ahead, mine, theirs))
            pieces[-k], pieces[k] = ahead, behind
        top = lax.ppermute(ahead[: shard // 2], "seq", up)
        bottom = lax.ppermute(behind[shard // 2 :], "seq", down)
        pieces[last] = jnp.concatenate([top, bottom], axis=0)

        theirs = lax.ppermute(theirs, "seq", flip)

        inner, outer = last // 2, last - 2
        groups = [
            list(range(-inner, inner + 1)),
            list(range(-outer, -inner)) + list(range(inner + 1, outer + 1)),
            [1 - last, last - 1, last],
        ]

        columns = 3 * width
        where = jnp.stack([z, half, core]).astype(jnp.int32)
        known = [(pieces[o], o, 0, shard) for o in groups[0] + groups[1]]
        kv = 2 * width
        inner_count = len(groups[0])
        full = (0, None, 0, columns, f32)
        sums = project(where, (mine,), (), known[:inner_count], [full], n_z, columns)
        (theirs_sum,) = project(where, (theirs,), (), known, [full], n_z, columns)
        full = (0, 0, 0, columns, f32)
        (mine_sum,) = project(where, (mine,), sums, known[inner_count:], [full], n_z, columns)
        final = jnp.concatenate([pieces[groups[2][0]], pieces[groups[2][1]], top, bottom], axis=0)

        def add_final(total, tok, lo, hi):
            picked = [lax.dynamic_index_in_dim(tok, (z + o + n_z) % n_z, 0, False) for o in groups[2]]
            part = lax.dot_general(
                jnp.concatenate(picked, axis=0),
                final[:, lo:hi],
                (((0,), (0,)), ((), ())),
                preferred_element_type=f32,
            )
            return total[:, lo:hi] + part

        sent = lax.ppermute(add_final(theirs_sum, theirs, 0, kv).astype(jnp.bfloat16), "seq", flip)
        kv_proj = add_final(mine_sum, mine, 0, kv) + sent.astype(f32)
        q_away = add_final(theirs_sum, theirs, kv, columns).astype(jnp.bfloat16)

        swaps, packs = [], []
        first, second = last // 2 - 1, last // 2 + 1
        batches = (
            list(range(-first, first + 1)),
            list(range(-second, -first)) + list(range(first + 1, second + 1)),
            list(range(1 - last, -second)) + list(range(second + 1, last + 1)),
        )
        for n, batch in enumerate(batches):
            packs.append(pack_outs([pieces[o] for o in batch], width))
            if n < 2:
                swaps.append(lax.ppermute(packs[n], "seq", flip))
            else:
                joined = jnp.concatenate([packs[n], q_away], axis=0)
                swaps.append(lax.ppermute(joined, "seq", flip))
        q_proj = add_final(mine_sum, mine, kv, columns) + swaps[2][packs[2].shape[0] :].astype(f32)

        key = jax.nn.silu(kv_proj[:, :width]).astype(jnp.bfloat16).reshape(rows, heads, hsize)
        value = kv_proj[:, width:].astype(jnp.bfloat16).reshape(rows, heads, hsize)
        query = jax.nn.silu(q_proj).astype(jnp.bfloat16).reshape(rows, heads, hsize)
        cum = jnp.cumsum(log_decay, axis=1)
        scaled_key = (key.astype(f32) * jnp.exp(cum[:, -1:] - cum).T[:, :, None]).astype(jnp.bfloat16)
        local = jnp.einsum("thd,the->hde", scaled_key, value, preferred_element_type=f32)
        earlier_state, where = exclusive_state(local, cum[:, -1], n_seq, where)
        outs = place_outs(where, packs, swaps, batches, n_z, shard, width)
        out_mine, out_theirs = outs[0], outs[1]

        later = jnp.arange(rows)[:, None] >= jnp.arange(rows)[None, :]
        scores = jnp.einsum("thd,shd->hts", query, key, preferred_element_type=f32)
        spread = cum[:, :, None] - cum[:, None, :]
        factor = jnp.where(later[None], jnp.exp(jnp.minimum(spread, 0.0)), 0.0)
        weights = (scores * factor).astype(jnp.bfloat16)
        intra = jnp.einsum("hts,shd->thd", weights, value, preferred_element_type=f32)
        intra = lax.optimization_barrier(intra)
        carried = jnp.einsum("thd,hde->the", query, earlier_state, preferred_element_type=f32)
        attn = intra + carried * jnp.exp(cum).T[:, :, None]
        power = jnp.mean(attn * attn, axis=-1, keepdims=True)
        gain = norm_gain.reshape(heads, hsize)
        normed = (attn / jnp.sqrt(power + 1e-05) * gain[None]).astype(jnp.bfloat16).reshape(rows, width)

        wide = jnp.broadcast_to(normed[None], (n_dp // 2, rows, width))
        give = jnp.einsum("itg,idg->itd", wide, out_theirs, preferred_element_type=f32)
        taken = lax.ppermute(give.astype(jnp.bfloat16), "dp", pair_perm(n_dp))
        keep = jnp.einsum("itg,idg->itd", wide, out_mine, preferred_element_type=f32)
        keep = lax.optimization_barrier(keep.astype(jnp.bfloat16)).astype(f32) + taken.astype(f32)
        groups = [[2 * i + c for i in range(n_dp // 2)] for c in range(2)]
        spread_out = lax.all_to_all(keep.astype(jnp.bfloat16), "dp", 0, 0, axis_index_groups=groups, tiled=True)
        return jnp.sum(spread_out.astype(f32), axis=0).astype(jnp.bfloat16)

    return layer


def solution(mesh):
    body = make_body(mesh.shape["seq"], mesh.shape["dp"])
    in_specs = (P("seq", None), P("seq", None, "dp"), P("seq", "dp"), P("dp", "seq"), P("dp"))
    return jax.shard_map(body, mesh=mesh, in_specs=in_specs, out_specs=P("seq", "dp"), check_vma=False)
```
